256 devices in a mesh: grp: 2 (over z_lo), tok: 64 (over y, x, z_hi), sub: 2 (over core).
Axes of the slice: x: 4, y: 4, z: 8 (z_hi: 4, z_lo: 2; z = z_hi * 2 + z_lo), core: 2. Of those that a mesh axis runs over, the one named last changes fastest.
Arguments:
- patches: bfloat16 [32768, 1408], P(('grp', 'tok')), may hold values from -6 to 6
- image_sizes: int32 [128, 4], P(('grp', 'tok')), may hold values from 1 to 32, 64 in all within a row
- vision_inproj: bfloat16 [1408, 2, 3, 704], P('tok', 'sub'), may hold values from -0.15625 to 0.15625
- vision_outproj: bfloat16 [1408, 1408], P('sub', 'tok'), may hold values from -0.625 to 0.625
- merger_weight: bfloat16 [5632, 1408], P('tok', 'sub'), may hold values from -0.078125 to 0.078125
- text_embed: bfloat16 [16384, 1408], P(('grp', 'tok')), may hold values from -6 to 6
- image_positions: int32 [2, 4096], P('grp', 'tok'), may hold values from 0 to 8191, as said below
- prompt_lengths: int32 [2, 2], P('grp'), may hold values from 1 to 8064, 8192 in all within a row
- decoder_inproj: bfloat16 [1408, 2, 3, 704], P(('grp', 'tok'), 'sub'), may hold values from -0.15625 to 0.15625
- decoder_outproj: bfloat16 [1408, 1408], P('sub', ('grp', 'tok')), may hold values from -0.625 to 0.625
Outputs:
- text_update: bfloat16 [16384, 1408], P(('grp', 'tok', 'sub'))
The draws below stay inside these ranges and needn't reach their ends.
Inputs may be any that keep to these rules, and one draw needn't show every extreme that they name: `image_positions`: within each half the positions are distinct. Of the 64 merged tokens of one piece, at most 2 go to positions of any one block of 128 positions, and some reach that number. `image_sizes`: each row sums to 64. `prompt_lengths`: each row sums to 8192.
All inputs are finite; a program needn't handle non-finite values.
Results may differ from the reference program's by a relative error of at most 0.03.
Values may be sent and summed in bfloat16 or wider, within the bound.
No kernel may reach another device: no remote copies, remote signals or barrier semaphores. Data moves between devices by JAX's collectives and lax.ppermute only.
A program may use at most 128 MiB of HBM per device.

```python
import math
import jax
import jax.numpy as jnp
import numpy as np
from jax import lax

HEADS = 16
HD = 88
D = 1408
VP = 256
PIECE = 128
IMGS = 4
REACH = 3
PROMPTS = 2
HALVES = 2
CHIPS = 128
PATCHES = 32768
G = 64
CAP = 2
TEXT_TOK = 16384
MAXLEN = 8064
N_TOK = 64
N_SUB = 2


def draw_image_positions(key, part):

    def one_half(half_key):
        split_keys = jax.random.split(half_key, 3)
        is_hot = (jax.random.permutation(split_keys[0], N_TOK) < N_TOK // 4).astype(jnp.int32)
        priority = jax.random.randint(split_keys[1], (N_TOK, N_TOK), 0, 1024) + is_hot[None, :] * 768
        scores = priority * N_TOK + jnp.arange(N_TOK, dtype=jnp.int32)[None, :]
        unused, chosen = lax.top_k(scores, N_TOK // 2)
        chosen = jnp.sort(chosen.astype(jnp.int32), axis=1)
        source = jnp.arange(N_TOK, dtype=jnp.int32)[:, None]
        member = jnp.zeros((N_TOK, N_TOK), jnp.int32).at[source, chosen].set(1)
        before = jnp.cumsum(member, axis=0) - member
        piece_load = jnp.sum(member, axis=0) * CAP
        offset = jax.random.randint(split_keys[2], (N_TOK,), 0, PIECE - piece_load + 1)
        token_index = jnp.arange(G, dtype=jnp.int32)
        target = chosen[:, token_index // CAP]
        position = target * PIECE + offset[target] + before[source, target] * CAP + token_index[None, :] % CAP
        return position.reshape(N_TOK * G).astype(jnp.int32)
    return jax.vmap(one_half)(jax.random.split(key, HALVES))


def block_scale(stream_key, shape, cuts, smallest, high):
    def one(dim, shards_of):
        steps = jax.random.uniform(jax.random.fold_in(jax.random.fold_in(stream_key, 6), dim), (shards_of,), jnp.float32, smallest / len(cuts), high / len(cuts))
        return jnp.repeat(jnp.exp(steps), shape[dim] // shards_of).reshape((-1,) + (1,) * (len(shape) - dim - 1))

    gain = one(*cuts[0])
    for cut in cuts[1:]:
        gain = gain * one(*cut)
    return gain


def length_profile(count, total, limit, slope):
    loads = [(1 << 20) // math.isqrt(rank ** slope) + 1 for rank in range(2, count + 1)]
    spare, counts = total - limit - (count - 1), [1] * (count - 1)
    while spare > 0:
        movable = [i for i in range(count - 1) if counts[i] < limit]
        whole, budget = sum([loads[i] for i in movable]), spare
        for i in movable:
            extra = min(limit - counts[i], max(1, budget * loads[i] // whole), spare)
            counts[i] = counts[i] + extra
            spare = spare - extra
    return np.array([limit] + counts)


def ragged(rng, amount, total, limit, skew):
    if amount == 2:
        one = jax.random.randint(rng, (), max(1, total - limit), min(limit, total - 1) + 1)
        return jnp.stack([one, total - one])
    tallies = jnp.asarray(length_profile(amount, total, limit, skew), jnp.int32)
    couples = (amount - 1) // 2
    giver, taker = tallies[1:1 + 2 * couples:2], tallies[2:2 + 2 * couples:2]
    margin = jnp.minimum(giver - 1, limit - taker)
    shifted = jax.random.randint(jax.random.fold_in(rng, 1), (couples,), 0, 1 << 20) % (margin + 1)
    tallies = tallies.at[1:1 + 2 * couples:2].set(giver - shifted).at[2:2 + 2 * couples:2].set(taker + shifted)
    return tallies[jax.random.permutation(jax.random.fold_in(rng, 2), amount)]


def bell_draw(stream_key, extent, scale, bound, shards=(), held_as=jnp.bfloat16):
    factor_of = block_scale(stream_key, extent, shards, -0.22, 0.18) if shards else 1.0
    result = jax.random.normal(stream_key, extent, jnp.float32) * scale * factor_of
    return jnp.minimum(jnp.maximum(result, -bound), bound).astype(held_as)


def setup_inputs(seed: int = 0) -> dict:
    arg_keys = jax.random.split(jax.random.key(seed), 11)
    return {
        "patches": bell_draw(arg_keys[0], (PATCHES, D), 1.0, 6.0, ((0, 128),)),
        "image_sizes": jax.vmap(lambda own: ragged(own, IMGS, G, G // 2, 2))(jax.random.split(arg_keys[1], CHIPS)).reshape((CHIPS, IMGS)).astype(jnp.int32),
        "vision_inproj": bell_draw(arg_keys[2], (D, N_SUB, 3, D // N_SUB), D ** -0.5, 0.15625, ((0, 64), (1, 2))),
        "vision_outproj": bell_draw(arg_keys[3], (D, D), HD ** -0.5, 0.625, ((0, 2), (1, 64))),
        "merger_weight": bell_draw(arg_keys[4], (4 * D, D), (4 * D) ** -0.5, 0.078125, ((0, 64), (1, 2))),
        "text_embed": bell_draw(arg_keys[5], (TEXT_TOK, D), 1.0, 6.0, ((0, 128),)),
        "image_positions": draw_image_positions(jax.random.fold_in(arg_keys[10], 71), 0),
        "prompt_lengths": jax.vmap(lambda own: ragged(own, PROMPTS, N_TOK * PIECE, MAXLEN, 2))(jax.random.split(arg_keys[7], HALVES)).reshape((HALVES, PROMPTS)).astype(jnp.int32),
        "decoder_inproj": bell_draw(arg_keys[8], (D, N_SUB, 3, D // N_SUB), D ** -0.5, 0.15625, ((0, 128), (1, 2))),
        "decoder_outproj": bell_draw(arg_keys[9], (D, D), HD ** -0.5, 0.625, ((0, 2), (1, 128))),
    }


norm_eps = 1e-06

def layer_norm(values):
    center = values - lax.optimization_barrier(jnp.mean(values, axis=-1, keepdims=True))
    spread = lax.optimization_barrier(jnp.mean(center * center, axis=-1, keepdims=True))
    return center * lax.rsqrt(spread + norm_eps)

def attend(queries, keys_all, values_all, allowed):
    scores = jnp.einsum('qhe,khe->hqk', queries.astype(jnp.float32), keys_all.astype(jnp.float32)) * (1.0 / math.sqrt(HD))
    weights_raw = jnp.exp(scores) * allowed[None]
    weights = (weights_raw / lax.optimization_barrier(jnp.sum(weights_raw, axis=-1, keepdims=True))).astype(jnp.bfloat16)
    mixture = jnp.einsum('hqk,khe->qhe', weights.astype(jnp.float32), values_all.astype(jnp.float32))
    return mixture.astype(jnp.bfloat16).reshape(queries.shape[0], D)

def split_heads(projected, row_total):
    triple = projected.astype(jnp.bfloat16).reshape(row_total, N_SUB, 3, D // N_SUB)
    return [triple[:, :, member].reshape(row_total, HEADS, HD) for member in range(3)]

def reference(patches, image_sizes, vision_inproj, vision_outproj, merger_weight, text_embed, image_positions, prompt_lengths, decoder_inproj, decoder_outproj):

    def vision_chip(chip_args):
        chip_patches, chip_sizes = chip_args
        patch_rows = chip_patches.astype(jnp.float32)
        normed = layer_norm(patch_rows).astype(jnp.bfloat16)
        projected = jnp.dot(normed, vision_inproj.reshape(D, 3 * D), preferred_element_type=jnp.float32)
        queries, keys_all, values_all = split_heads(projected, VP)
        image_ends = jnp.cumsum(chip_sizes)
        group_ids = jnp.arange(VP, dtype=jnp.int32) // 4
        image_ids = lax.optimization_barrier(jnp.sum((group_ids[:, None] >= image_ends[None, :]).astype(jnp.int32), axis=1))
        same_image = (image_ids[:, None] == image_ids[None, :]).astype(jnp.float32)
        heads_out = attend(queries, keys_all, values_all, same_image)
        hidden = patch_rows + jnp.dot(heads_out, vision_outproj, preferred_element_type=jnp.float32)
        merged = layer_norm(hidden).astype(jnp.bfloat16).reshape(VP // 4, 4 * D)
        return jnp.dot(merged, merger_weight, preferred_element_type=jnp.float32).astype(jnp.bfloat16)
    images = lax.map(vision_chip, (patches.reshape(CHIPS, VP, D), image_sizes))
    half_rows = N_TOK * PIECE
    window_rows = (REACH + 1) * PIECE
    outputs = []
    for half_index in range(HALVES):
        text_rows = text_embed[half_index * half_rows:(half_index + 1) * half_rows]
        half_images = images[half_index * N_TOK:(half_index + 1) * N_TOK].reshape(N_TOK * (VP // 4), D)
        decoder_input = text_rows.at[image_positions[half_index]].set(half_images)
        normed = layer_norm(decoder_input.astype(jnp.float32)).astype(jnp.bfloat16)
        projected = jnp.dot(normed, decoder_inproj.reshape(D, 3 * D), preferred_element_type=jnp.float32)
        queries, keys_all, values_all = split_heads(projected, half_rows)
        front = jnp.zeros((REACH * PIECE, HEADS, HD), jnp.bfloat16)
        padded_keys = jnp.concatenate([front, keys_all], axis=0)
        padded_values = jnp.concatenate([front, values_all], axis=0)
        lengths = prompt_lengths[half_index]
        starts = jnp.cumsum(lengths) - lengths

        def one_piece(piece_index):
            query_pos = piece_index * PIECE + jnp.arange(PIECE, dtype=jnp.int32)
            key_pos = (piece_index - REACH) * PIECE + jnp.arange(window_rows, dtype=jnp.int32)
            query_start = lax.optimization_barrier(jnp.max(jnp.where(starts[None, :] <= query_pos[:, None], starts[None, :], 0), axis=1))
            allowed = ((key_pos[None, :] <= query_pos[:, None]) & (key_pos[None, :] >= query_start[:, None])).astype(jnp.float32)
            piece_queries = lax.dynamic_slice_in_dim(queries, piece_index * PIECE, PIECE, 0)
            piece_keys = lax.dynamic_slice_in_dim(padded_keys, piece_index * PIECE, window_rows, 0)
            piece_values = lax.dynamic_slice_in_dim(padded_values, piece_index * PIECE, window_rows, 0)
            return attend(piece_queries, piece_keys, piece_values, allowed)
        heads_out = lax.map(one_piece, jnp.arange(N_TOK, dtype=jnp.int32)).reshape(half_rows, D)
        outputs.append(jnp.dot(heads_out, decoder_outproj, preferred_element_type=jnp.float32).astype(jnp.bfloat16))
    return jnp.concatenate(outputs, axis=0)
```

```python
import math

import jax
import jax.numpy as jnp
from jax import lax
from jax.sharding import Mesh
from jax.sharding import PartitionSpec as P

HD = 88
REACH = 3
EPS = 1e-06
TOK = ("y", "x", "zh")
PLANE = ("y", "x")
BF = jnp.bfloat16
F32 = jnp.float32


def layer_norm(values):
    center = values - jnp.mean(values, axis=-1, keepdims=True)
    spread = jnp.mean(center * center, axis=-1, keepdims=True)
    return center * lax.rsqrt(spread + EPS)


def softmax_weights(scores, allowed):
    raw = jnp.exp(scores * (1.0 / math.sqrt(HD))) * allowed
    return (raw / jnp.sum(raw, axis=-1, keepdims=True)).astype(BF)


def after(value, *others):
    return lax.optimization_barrier((value, *others))[0]


def swap_sub(value):
    return lax.ppermute(value, "sub", [(0, 1), (1, 0)])


def dot(a, b):
    return jnp.dot(a, b, preferred_element_type=F32)


def to_all(value, axes):
    count = lax.axis_size(axes)
    spread = jnp.broadcast_to(value[None], (count,) + value.shape)
    return lax.all_to_all(spread, axes, split_axis=0, concat_axis=0, tiled=True)


def shards(
    patches,
    image_sizes,
    vision_inproj,
    vision_outproj,
    merger_weight,
    text_embed,
    image_positions,
    prompt_lengths,
    decoder_inproj,
    decoder_outproj,
):
    lines = lax.axis_size("zh")
    planes = lax.axis_size(PLANE)
    pieces = lax.axis_size(TOK)
    rows_v, width = patches.shape
    half = vision_inproj.shape[3]
    quarter = half // lines
    heads_line = quarter // HD
    krows = vision_inproj.shape[0]
    mrows = merger_weight.shape[0]

    vin = vision_inproj.reshape(krows, 3, lines, quarter).transpose(2, 0, 1, 3)
    vin = vin.reshape(lines, krows, 3 * quarter)
    vin = jnp.pad(vin, ((0, 0), (0, 0), (0, half - 3 * quarter)))
    rest = jnp.concatenate([vision_outproj.T, merger_weight], axis=0)
    rest = jnp.broadcast_to(rest[None], (lines,) + rest.shape)
    line_v = lax.all_to_all(
        jnp.concatenate([vin, rest], axis=1), "zh", split_axis=0, concat_axis=0, tiled=True
    )
    line_v = jnp.concatenate(
        [
            line_v[:, :krows].reshape(lines * krows, half),
            line_v[:, krows : 2 * krows].reshape(lines * krows, half),
            line_v[:, 2 * krows :].reshape(lines * mrows, half),
        ],
        axis=0,
    )
    full_v = lax.all_gather(line_v, PLANE, axis=0, tiled=False)
    kline = lines * krows
    w_in = full_v[:, :kline].reshape(width, half)
    w_out = full_v[:, kline : 2 * kline].reshape(width, half)
    w_merge = full_v[:, 2 * kline :].reshape(planes * lines * mrows, half)

    drows = decoder_inproj.shape[0]
    dec = jnp.concatenate([decoder_inproj.reshape(drows, 3 * half), decoder_outproj.T], axis=1)
    dec = after(dec, line_v)
    line_d = to_all(dec, ("grp", "zh")).reshape(-1, 4 * half)
    full_d = lax.all_gather(line_d, PLANE, axis=0, tiled=True)
    fan = lines * drows
    order = jnp.arange(width, dtype=jnp.int32)
    natural = (
        (order // fan) % 2 * (width // 2) + order // (2 * fan) * fan + order % fan
    )
    reorder = (natural[None, :] == order[:, None]).astype(BF)

    piece_rows = text_embed.shape[0]
    reach = REACH + 1
    cap = rows_v // (2 * pieces)
    slots = reach * cap
    targets = image_positions[0]
    target_piece = targets // piece_rows
    target_row = targets % piece_rows
    hits = (target_piece[:, None] == jnp.arange(pieces, dtype=jnp.int32)[None, :]).astype(jnp.int32)
    slot = jnp.sum((jnp.cumsum(hits, axis=0) - hits) * hits, axis=1)
    dest = jnp.arange(pieces * slots, dtype=jnp.int32)
    back = dest // cap % reach
    wanted = (dest // slots)[:, None] - back[:, None] == target_piece[None, :]
    wanted = wanted & ((dest % cap)[:, None] == slot[None, :])
    window_row = (REACH - back)[:, None] * piece_rows + target_row[None, :]
    window_rows = reach * piece_rows
    row_list = jnp.min(jnp.where(wanted, window_row, window_rows), axis=1)
    row_list = after(row_list.reshape(pieces, slots), line_d)
    arrived = lax.all_to_all(row_list, TOK, split_axis=0, concat_axis=0, tiled=True).reshape(-1)
    place = jnp.arange(window_rows, dtype=jnp.int32)[:, None] == arrived[None, :]

    patch_rows = patches.astype(F32)
    ends = jnp.cumsum(image_sizes[0]).astype(BF)
    mark = jnp.zeros((16, width), BF).at[0, : ends.shape[0]].set(ends)
    own = jnp.concatenate([layer_norm(patch_rows).astype(BF), mark], axis=0)
    own = after(own, arrived)
    moved = [
        lax.ppermute(own, "zh", [(i, (i + s) % lines) for i in range(lines)])
        for s in range(1, lines)
    ]
    text = after(text_embed, moved[0])
    earlier = [
        lax.ppermute(text, TOK, [(i, i + s) for i in range(pieces - s)])
        for s in range(REACH, 0, -1)
    ]
    window_text = jnp.concatenate(earlier + [text_embed], axis=0)

    both = jnp.stack([own] + moved)
    normed = both[:, :rows_v].reshape(lines * rows_v, width)
    ends_all = both[:, rows_v, : ends.shape[0]].astype(jnp.int32)
    group_ids = jnp.arange(rows_v, dtype=jnp.int32) // 4
    image_ids = jnp.sum(
        (group_ids[None, :, None] >= ends_all[:, None, :]).astype(jnp.int32), axis=2
    )
    same = (image_ids[:, :, None] == image_ids[:, None, :]).astype(F32)
    projected = dot(normed, w_in)[:, : 3 * quarter].astype(BF)
    triple = projected.reshape(lines, rows_v, 3, heads_line, HD)
    scores = jnp.einsum(
        "pqhe,pkhe->phqk", triple[:, :, 0], triple[:, :, 1], preferred_element_type=F32
    )
    weights = softmax_weights(scores, same[:, None])
    heads = jnp.einsum("phqk,pkhe->pqhe", weights, triple[:, :, 2], preferred_element_type=F32)
    heads = heads.astype(BF).reshape(lines, rows_v, quarter)
    me = lax.axis_index("zh")
    heads = jnp.roll(heads[::-1], me + 1, axis=0)
    heads = lax.all_to_all(heads, "zh", split_axis=0, concat_axis=0, tiled=True)
    heads = heads.transpose(1, 0, 2).reshape(rows_v, half)
    partial = lax.dot_general(heads, w_out, (((1,), (1,)), ((), ())), preferred_element_type=F32)
    partial = partial.astype(BF)
    hidden = patch_rows + (partial.astype(F32) + swap_sub(partial).astype(F32))
    merged = layer_norm(hidden).astype(BF).reshape(rows_v // 4, 4 * width)
    embedded = dot(merged, w_merge).astype(BF)

    sent = dot(wanted.astype(BF), embedded).astype(BF).reshape(pieces, slots, half)
    got = lax.all_to_all(sent, TOK, split_axis=0, concat_axis=0, tiled=True)
    got = got.reshape(pieces * slots, half)
    other = swap_sub(got)
    first = lax.axis_index("sub") == 0
    image_full = jnp.concatenate(
        [jnp.where(first, got, other), jnp.where(first, other, got)], axis=1
    )
    placed = dot(place.astype(BF), image_full)
    filled = jnp.any(place, axis=1)
    decoder_input = jnp.where(filled[:, None], placed, window_text.astype(F32))
    normed_text = layer_norm(decoder_input).astype(BF)
    normed_text = dot(normed_text, reorder).astype(BF)
    head_local = half // HD
    query = dot(normed_text[REACH * piece_rows :], full_d[:, :half]).astype(BF)
    pair = dot(normed_text, full_d[:, half : 3 * half]).astype(BF)
    query = query.reshape(piece_rows, head_local, HD)
    pair = pair.reshape(window_rows, 2, head_local, HD)

    piece_id = lax.axis_index(TOK)
    query_pos = piece_id * piece_rows + jnp.arange(piece_rows, dtype=jnp.int32)
    key_pos = (piece_id - REACH) * piece_rows + jnp.arange(window_rows, dtype=jnp.int32)
    lengths = prompt_lengths[0]
    starts = jnp.cumsum(lengths) - lengths
    query_start = jnp.max(
        jnp.where(starts[None, :] <= query_pos[:, None], starts[None, :], 0), axis=1
    )
    allowed = (
        (key_pos[None, :] <= query_pos[:, None]) & (key_pos[None, :] >= query_start[:, None])
    ).astype(F32)
    scores = jnp.einsum("qhe,khe->hqk", query, pair[:, 0], preferred_element_type=F32)
    weights = softmax_weights(scores, allowed[None])
    text_heads = jnp.einsum("hqk,khe->qhe", weights, pair[:, 1], preferred_element_type=F32)
    text_heads = text_heads.astype(BF).reshape(piece_rows, half)
    partial = lax.dot_general(
        text_heads, full_d[:, 3 * half :], (((1,), (1,)), ((), ())), preferred_element_type=F32
    ).astype(BF)
    sub = lax.axis_index("sub")
    keep_rows = piece_rows // 2
    give = lax.dynamic_slice_in_dim(partial, (1 - sub) * keep_rows, keep_rows, 0)
    keep = lax.dynamic_slice_in_dim(partial, sub * keep_rows, keep_rows, 0)
    total = (keep.astype(F32) + swap_sub(give).astype(F32)).astype(BF)
    return lax.dot_general(
        total, reorder, (((1,), (1,)), ((), ())), preferred_element_type=F32
    ).astype(BF)


def solution(mesh):
    grp, tok, sub = mesh.devices.shape
    lined = Mesh(mesh.devices.reshape(grp, 4, 4, tok // 16, sub), ("grp", "y", "x", "zh", "sub"))
    whole = ("grp",) + TOK
    placed = (
        P(whole, None),
        P(whole, None),
        P(TOK, "sub", None, None),
        P("sub", TOK),
        P(TOK, "sub"),
        P(whole, None),
        P("grp", TOK),
        P("grp", None),
        P(whole, "sub", None, None),
        P("sub", whole),
    )
    return jax.shard_map(
        shards,
        mesh=lined,
        in_specs=placed,
        out_specs=P(whole + ("sub",), None),
        check_vma=False,
    )
```

```python
import math

import jax
import jax.numpy as jnp
from jax import lax
from jax.sharding import Mesh
from jax.sharding import PartitionSpec as P

HD = 88
REACH = 3
EPS = 1e-06
TOK = ("y", "x", "zh")
PLANE = ("y", "x")
BF = jnp.bfloat16
F32 = jnp.float32


def layer_norm(values):
    center = values - jnp.mean(values, axis=-1, keepdims=True)
    spread = jnp.mean(center * center, axis=-1, keepdims=True)
    return center * lax.rsqrt(spread + EPS)


def softmax_weights(scores, allowed):
    raw = jnp.exp(scores * (1.0 / math.sqrt(HD))) * allowed
    return (raw / jnp.sum(raw, axis=-1, keepdims=True)).astype(BF)


def swap_sub(value):
    return lax.ppermute(value, "sub", [(0, 1), (1, 0)])


def dot(a, b):
    return jnp.dot(a, b, preferred_element_type=F32)


def to_all(value, axes):
    count = lax.axis_size(axes)
    spread = jnp.broadcast_to(value[None], (count,) + value.shape)
    return lax.all_to_all(spread, axes, split_axis=0, concat_axis=0, tiled=True)


def shards(
    patches,
    image_sizes,
    vision_inproj,
    vision_outproj,
    merger_weight,
    text_embed,
    image_positions,
    prompt_lengths,
    decoder_inproj,
    decoder_outproj,
):
    lines = lax.axis_size("zh")
    planes = lax.axis_size(PLANE)
    pieces = lax.axis_size(TOK)
    rows_v, width = patches.shape
    half = vision_inproj.shape[3]
    quarter = half // lines
    heads_line = quarter // HD
    krows = vision_inproj.shape[0]
    mrows = merger_weight.shape[0]

    line_m = to_all(merger_weight, "zh").reshape(lines * mrows, half)

    vin = vision_inproj.reshape(krows, 3, lines, quarter).transpose(2, 0, 1, 3)
    vin = vin.reshape(lines, krows, 3 * quarter)
    vin = jnp.pad(vin, ((0, 0), (0, 0), (0, half - 3 * quarter)))
    drows = decoder_inproj.shape[0]
    dec = jnp.concatenate(
        [decoder_inproj.reshape(drows, 3, half).transpose(1, 0, 2), decoder_outproj.T[None]], axis=0
    )
    dec_other = lax.ppermute(dec, "grp", [(0, 1), (1, 0)])
    low = lax.axis_index("grp") == 0
    dec = jnp.stack([jnp.where(low, dec, dec_other), jnp.where(low, dec_other, dec)], axis=1)
    rest = jnp.concatenate([vision_outproj.T, dec.reshape(8 * drows, half)], axis=0)
    rest = jnp.broadcast_to(rest[None], (lines,) + rest.shape)
    line = jnp.concatenate([vin, rest], axis=1)
    line, line_m = lax.optimization_barrier((line, line_m))
    w_merge = lax.all_gather(line_m, PLANE, axis=0, tiled=True)
    line = lax.all_to_all(line, "zh", split_axis=0, concat_axis=0, tiled=True)
    kline = lines * krows
    line_v = jnp.concatenate(
        [
            line[:, :krows, : 3 * quarter].reshape(kline, 3 * quarter),
            line[:, krows : 2 * krows].reshape(kline, half),
        ],
        axis=1,
    )
    line_d = line[:, 2 * krows :].reshape(lines, 4, 2 * drows, half).transpose(0, 2, 1, 3)
    line_d = line_d.reshape(lines * 2 * drows, 4 * half)
    full_d = lax.all_gather(line_d, PLANE, axis=0, tiled=True)
    full_v = to_all(line_v, PLANE).reshape(width, 3 * quarter + half)
    w_in = full_v[:, : 3 * quarter]
    w_out = full_v[:, 3 * quarter :]
    order = jnp.arange(width, dtype=jnp.int32)
    natural = (
        order // drows % 2 * (width // 2) + order // (2 * drows) * drows + order % drows
    )
    reorder = (natural[None, :] == order[:, None]).astype(BF)

    piece_rows = text_embed.shape[0]
    reach = REACH + 1
    cap = rows_v // (2 * pieces)
    slots = reach * cap
    targets = image_positions[0]
    target_piece = targets // piece_rows
    target_row = targets % piece_rows
    hits = (target_piece[:, None] == jnp.arange(pieces, dtype=jnp.int32)[None, :]).astype(jnp.int32)
    slot = jnp.sum((jnp.cumsum(hits, axis=0) - hits) * hits, axis=1)
    dest = jnp.arange(pieces * slots, dtype=jnp.int32)
    back = dest // cap % reach
    wanted = (dest // slots)[:, None] - back[:, None] == target_piece[None, :]
    wanted = wanted & ((dest % cap)[:, None] == slot[None, :])
    window_rows = reach * piece_rows

    patch_rows = patches.astype(F32)
    first = lax.axis_index("sub") == 0
    ends = jnp.cumsum(image_sizes[0]).astype(BF)
    mark = jnp.zeros((16, width), BF).at[0, : ends.shape[0]].set(ends)
    normed = layer_norm(patch_rows).astype(BF)
    side = rows_v // 2
    top, bottom = normed[:side], normed[side:]
    mine = jnp.concatenate([jnp.where(first, top, bottom), mark], axis=0)
    moved = [
        lax.ppermute(mine, "zh", [(i, (i + s) % lines) for i in range(lines)])
        for s in range(1, lines)
    ]
    moved = jnp.stack(moved)
    traded = swap_sub(moved[:, :side])
    kept = moved[:, :side]
    others = jnp.concatenate(
        [jnp.where(first, kept, traded), jnp.where(first, traded, kept)], axis=1
    )
    text, others = lax.optimization_barrier((text_embed, others))
    earlier = [
        lax.ppermute(text, TOK, [(i, i + s) for i in range(pieces - s)])
        for s in range(REACH, 0, -1)
    ]
    window_text = jnp.concatenate(earlier + [text], axis=0)

    normed = jnp.concatenate([normed[None], others]).reshape(lines * rows_v, width)
    ends_all = jnp.concatenate([ends[None], moved[:, side, : ends.shape[0]]]).astype(jnp.int32)
    group_ids = jnp.arange(rows_v, dtype=jnp.int32) // 4
    image_ids = jnp.sum(
        (group_ids[None, :, None] >= ends_all[:, None, :]).astype(jnp.int32), axis=2
    )
    same = (image_ids[:, :, None] == image_ids[:, None, :]).astype(F32)
    projected = dot(normed, w_in).astype(BF)
    triple = projected.reshape(lines, rows_v, 3, heads_line, HD)
    scores = jnp.einsum(
        "pqhe,pkhe->phqk", triple[:, :, 0], triple[:, :, 1], preferred_element_type=F32
    )
    weights = softmax_weights(scores, same[:, None])
    heads = jnp.einsum("phqk,pkhe->pqhe", weights, triple[:, :, 2], preferred_element_type=F32)
    heads = heads.astype(BF).reshape(lines, rows_v, quarter)
    me = lax.axis_index("zh")
    heads = jnp.roll(heads[::-1], me + 1, axis=0)
    heads, window_text = lax.optimization_barrier((heads, window_text))
    heads = lax.all_to_all(heads, "zh", split_axis=0, concat_axis=0, tiled=True)
    heads = heads.transpose(1, 0, 2).reshape(rows_v, half)
    partial = lax.dot_general(heads, w_out, (((1,), (1,)), ((), ())), preferred_element_type=F32)
    partial = partial.astype(BF)
    hidden = patch_rows + (partial.astype(F32) + swap_sub(partial).astype(F32))
    merged = layer_norm(hidden).astype(BF).reshape(rows_v // 4, 4 * width)
    embedded = dot(merged, w_merge).astype(BF)

    note = jnp.stack([target_row, jnp.ones_like(target_row)], axis=1).astype(BF)
    note = jnp.pad(note, ((0, 0), (0, 62)))
    sent = dot(wanted.astype(BF), jnp.concatenate([embedded, note], axis=1)).astype(BF)
    got = lax.all_to_all(
        sent.reshape(pieces, slots, half + 64), TOK, split_axis=0, concat_axis=0, tiled=True
    ).reshape(pieces * slots, half + 64)
    note = got[:, half : half + 2].astype(jnp.int32)
    arrived = jnp.arange(pieces * slots, dtype=jnp.int32) // cap % reach
    arrived = jnp.where(note[:, 1] > 0, (REACH - arrived) * piece_rows + note[:, 0], window_rows)
    place = jnp.arange(window_rows, dtype=jnp.int32)[:, None] == arrived[None, :]
    got = got[:, :half]
    other = swap_sub(got)
    image_full = jnp.concatenate(
        [jnp.where(first, got, other), jnp.where(first, other, got)], axis=1
    )
    placed = dot(place.astype(BF), image_full)
    filled = jnp.any(place, axis=1)
    decoder_input = jnp.where(filled[:, None], placed, window_text.astype(F32))
    normed_text = layer_norm(decoder_input).astype(BF)
    normed_text = dot(normed_text, reorder).astype(BF)
    head_local = half // HD
    query = dot(normed_text[REACH * piece_rows :], full_d[:, :half]).astype(BF)
    pair = dot(normed_text, full_d[:, half : 3 * half]).astype(BF)
    query = query.reshape(piece_rows, head_local, HD)
    pair = pair.reshape(window_rows, 2, head_local, HD)

    piece_id = lax.axis_index(TOK)
    query_pos = piece_id * piece_rows + jnp.arange(piece_rows, dtype=jnp.int32)
    key_pos = (piece_id - REACH) * piece_rows + jnp.arange(window_rows, dtype=jnp.int32)
    lengths = prompt_lengths[0]
    starts = jnp.cumsum(lengths) - lengths
    query_start = jnp.max(
        jnp.where(starts[None, :] <= query_pos[:, None], starts[None, :], 0), axis=1
    )
    allowed = (
        (key_pos[None, :] <= query_pos[:, None]) & (key_pos[None, :] >= query_start[:, None])
    ).astype(F32)
    scores = jnp.einsum("qhe,khe->hqk", query, pair[:, 0], preferred_element_type=F32)
    weights = softmax_weights(scores, allowed[None])
    text_heads = jnp.einsum("hqk,khe->qhe", weights, pair[:, 1], preferred_element_type=F32)
    text_heads = text_heads.astype(BF).reshape(piece_rows, half)
    partial = lax.dot_general(
        text_heads, full_d[:, 3 * half :], (((1,), (1,)), ((), ())), preferred_element_type=F32
    ).astype(BF)
    sub = lax.axis_index("sub")
    keep_rows = piece_rows // 2
    give = lax.dynamic_slice_in_dim(partial, (1 - sub) * keep_rows, keep_rows, 0)
    keep = lax.dynamic_slice_in_dim(partial, sub * keep_rows, keep_rows, 0)
    total = (keep.astype(F32) + swap_sub(give).astype(F32)).astype(BF)
    return lax.dot_general(
        total, reorder, (((1,), (1,)), ((), ())), preferred_element_type=F32
    ).astype(BF)


def solution(mesh):
    grp, tok, sub = mesh.devices.shape
    lined = Mesh(mesh.devices.reshape(grp, 4, 4, tok // 16, sub), ("grp", "y", "x", "zh", "sub"))
    whole = ("grp",) + TOK
    placed = (
        P(whole, None),
        P(whole, None),
        P(TOK, "sub", None, None),
        P("sub", TOK),
        P(TOK, "sub"),
        P(whole, None),
        P("grp", TOK),
        P("grp", None),
        P(whole, "sub", None, None),
        P("sub", whole),
    )
    return jax.shard_map(
        shards,
        mesh=lined,
        in_specs=placed,
        out_specs=P(whole + ("sub",), None),
        check_vma=False,
    )
```

```python
import math

import jax
import jax.numpy as jnp
from jax import lax
from jax.sharding import Mesh
from jax.sharding import PartitionSpec as P

HD = 88
REACH = 3
EPS = 1e-06
TOK = ("y", "x", "zh")
PLANE = ("y", "x")
BF = jnp.bfloat16
F32 = jnp.float32


def layer_norm(values):
    center = values - jnp.mean(values, axis=-1, keepdims=True)
    spread = jnp.mean(center * center, axis=-1, keepdims=True)
    return center * lax.rsqrt(spread + EPS)


def softmax_weights(scores, allowed):
    raw = jnp.exp(scores * (1.0 / math.sqrt(HD))) * allowed
    return (raw / jnp.sum(raw, axis=-1, keepdims=True)).astype(BF)


def swap_sub(value):
    return lax.ppermute(value, "sub", [(0, 1), (1, 0)])


def dot(a, b):
    return jnp.dot(a, b, preferred_element_type=F32)


def both_halves(part, first):
    other = swap_sub(part)
    return jnp.concatenate(
        [jnp.where(first, part, other), jnp.where(first, other, part)], axis=1
    )


def pad_to(columns):
    return -columns % 128


def to_all(value, axes):
    count = lax.axis_size(axes)
    spread = jnp.broadcast_to(value[None], (count,) + value.shape)
    return lax.all_to_all(spread, axes, split_axis=0, concat_axis=0, tiled=True)


def shards(
    patches,
    image_sizes,
    vision_inproj,
    vision_outproj,
    merger_weight,
    text_embed,
    image_positions,
    prompt_lengths,
    decoder_inproj,
    decoder_outproj,
):
    lines = lax.axis_size("zh")
    planes = lax.axis_size(PLANE)
    pieces = lax.axis_size(TOK)
    rows_v, width = patches.shape
    half = vision_inproj.shape[3]
    quarter = half // lines
    heads_line = quarter // HD
    krows = vision_inproj.shape[0]
    mrows = merger_weight.shape[0]

    vin = vision_inproj.reshape(krows, 3, lines, quarter).transpose(2, 0, 1, 3)
    vin = vin.reshape(lines, krows, 3 * quarter)
    vin = jnp.pad(vin, ((0, 0), (0, 0), (0, pad_to(3 * quarter))))
    vout = jnp.pad(vision_outproj.T, ((0, 0), (0, pad_to(half))))
    vout = jnp.broadcast_to(vout[None], (lines,) + vout.shape)
    line = jnp.concatenate([vin, vout], axis=2)
    line = lax.all_to_all(line, "zh", split_axis=0, concat_axis=0, tiled=True)
    split_out = vin.shape[2]
    split_merge = line.shape[2]
    line_v = line.reshape(lines * krows, split_merge)
    merge = jnp.pad(merger_weight, ((0, 0), (0, pad_to(half))))
    line_v = jnp.concatenate([line_v, merge], axis=1)

    drows = decoder_inproj.shape[0]
    dec = jnp.concatenate(
        [decoder_inproj.reshape(drows, 3, half).transpose(1, 0, 2), decoder_outproj.T[None]], axis=0
    )
    dec_other = lax.ppermute(dec, "grp", [(0, 1), (1, 0)])
    low = lax.axis_index("grp") == 0
    dec = jnp.stack([jnp.where(low, dec, dec_other), jnp.where(low, dec_other, dec)], axis=1)
    dec = dec.reshape(8 * drows, half)
    patch_rows = patches.astype(F32)
    normed = layer_norm(patch_rows).astype(BF)
    line_v, dec, normed = lax.optimization_barrier((line_v, dec, normed))
    full_v = lax.all_gather(line_v, PLANE, axis=0, tiled=True)
    line_d = to_all(dec, "zh").reshape(lines, 4, 2 * drows, half).transpose(0, 2, 1, 3)
    line_d = line_d.reshape(lines * 2 * drows, 4 * half)
    full_d = lax.all_gather(line_d, PLANE, axis=0, tiled=True)
    order = jnp.arange(width, dtype=jnp.int32)
    natural = (
        order // drows % 2 * (width // 2) + order // (2 * drows) * drows + order % drows
    )
    reorder = (natural[None, :] == order[:, None]).astype(BF)

    piece_rows = text_embed.shape[0]
    reach = REACH + 1
    cap = rows_v // (2 * pieces)
    slots = reach * cap
    targets = image_positions[0]
    target_piece = targets // piece_rows
    target_row = targets % piece_rows
    hits = (target_piece[:, None] == jnp.arange(pieces, dtype=jnp.int32)[None, :]).astype(jnp.int32)
    slot = jnp.sum((jnp.cumsum(hits, axis=0) - hits) * hits, axis=1)
    dest = jnp.arange(pieces * slots, dtype=jnp.int32)
    back = dest // cap % reach
    wanted = (dest // slots)[:, None] - back[:, None] == target_piece[None, :]
    wanted = wanted & ((dest % cap)[:, None] == slot[None, :])
    window_rows = reach * piece_rows

    first = lax.axis_index("sub") == 0
    ends = jnp.cumsum(image_sizes[0]).astype(BF)
    mark = jnp.zeros((16, width), BF).at[0, : ends.shape[0]].set(ends)
    side = rows_v // 2
    mine = jnp.concatenate([jnp.where(first, normed[:side], normed[side:]), mark], axis=0)
    moved = jnp.stack(
        [
            lax.ppermute(mine, "zh", [(i, (i + s) % lines) for i in range(lines)])
            for s in range(1, lines)
        ]
    )
    others = both_halves(moved[:, :side], first)
    text, others, reorder = lax.optimization_barrier((text_embed, others, reorder))
    side_t = piece_rows // 2
    mine = jnp.where(first, text[:side_t], text[side_t:])
    earlier = jnp.stack(
        [
            lax.ppermute(mine, TOK, [(i, i + s) for i in range(pieces - s)])
            for s in range(REACH, 0, -1)
        ]
    )
    earlier = both_halves(earlier, first).reshape(REACH * piece_rows, width)
    window_text = jnp.concatenate([earlier, text], axis=0)

    normed = jnp.concatenate([normed[None], others]).reshape(lines * rows_v, width)
    ends_all = jnp.concatenate([ends[None], moved[:, side, : ends.shape[0]]]).astype(jnp.int32)
    group_ids = jnp.arange(rows_v, dtype=jnp.int32) // 4
    image_ids = jnp.sum(
        (group_ids[None, :, None] >= ends_all[:, None, :]).astype(jnp.int32), axis=2
    )
    same = (image_ids[:, :, None] == image_ids[:, None, :]).astype(F32)
    projected = dot(normed, full_v[:, : 3 * quarter]).astype(BF)
    triple = projected.reshape(lines, rows_v, 3, heads_line, HD)
    scores = jnp.einsum(
        "pqhe,pkhe->phqk", triple[:, :, 0], triple[:, :, 1], preferred_element_type=F32
    )
    weights = softmax_weights(scores, same[:, None])
    heads = jnp.einsum("phqk,pkhe->pqhe", weights, triple[:, :, 2], preferred_element_type=F32)
    heads = heads.astype(BF).reshape(lines, rows_v, quarter)
    me = lax.axis_index("zh")
    heads = jnp.roll(heads[::-1], me + 1, axis=0)
    heads, window_text = lax.optimization_barrier((heads, window_text))
    heads = lax.all_to_all(heads, "zh", split_axis=0, concat_axis=0, tiled=True)
    heads = heads.transpose(1, 0, 2).reshape(rows_v, half)
    w_out = full_v[:, split_out : split_out + half]
    partial = lax.dot_general(heads, w_out, (((1,), (1,)), ((), ())), preferred_element_type=F32)
    partial = partial.astype(BF)
    hidden = patch_rows + (partial.astype(F32) + swap_sub(partial).astype(F32))
    tokens = rows_v // 4
    merged = layer_norm(hidden).astype(BF).reshape(tokens, planes, lines, mrows)
    merged = merged.transpose(2, 0, 1, 3).reshape(lines, tokens, planes * mrows)
    merged = lax.all_to_all(merged, "zh", split_axis=0, concat_axis=0, tiled=True)
    partial = dot(merged.reshape(lines * tokens, planes * mrows), full_v[:, split_merge : split_merge + half])
    partial = partial.astype(BF).reshape(lines, tokens, half)
    partial = lax.all_to_all(partial, "zh", split_axis=0, concat_axis=0, tiled=True)
    embedded = jnp.sum(partial.astype(F32), axis=0).astype(BF)

    note = jnp.stack([target_row, jnp.ones_like(target_row)], axis=1).astype(BF)
    note = jnp.pad(note, ((0, 0), (0, pad_to(half) - 2)))
    sent = dot(wanted.astype(BF), jnp.concatenate([embedded, note], axis=1)).astype(BF)
    got = lax.all_to_all(
        sent.reshape(pieces, slots, half + pad_to(half)), TOK, split_axis=0, concat_axis=0, tiled=True
    ).reshape(pieces * slots, half + pad_to(half))
    note = got[:, half : half + 2].astype(jnp.int32)
    arrived = jnp.arange(pieces * slots, dtype=jnp.int32) // cap % reach
    arrived = jnp.where(note[:, 1] > 0, (REACH - arrived) * piece_rows + note[:, 0], window_rows)
    place = jnp.arange(window_rows, dtype=jnp.int32)[:, None] == arrived[None, :]
    got = got[:, :half]
    image_full = both_halves(got, first)
    placed = dot(place.astype(BF), image_full)
    filled = jnp.any(place, axis=1)
    decoder_input = jnp.where(filled[:, None], placed, window_text.astype(F32))
    normed_text = layer_norm(decoder_input).astype(BF)
    normed_text = dot(normed_text, reorder).astype(BF)
    head_local = half // HD
    query = dot(normed_text[REACH * piece_rows :], full_d[:, :half]).astype(BF)
    pair = dot(normed_text, full_d[:, half : 3 * half]).astype(BF)
    query = query.reshape(piece_rows, head_local, HD)
    pair = pair.reshape(window_rows, 2, head_local, HD)

    piece_id = lax.axis_index(TOK)
    query_pos = piece_id * piece_rows + jnp.arange(piece_rows, dtype=jnp.int32)
    key_pos = (piece_id - REACH) * piece_rows + jnp.arange(window_rows, dtype=jnp.int32)
    lengths = prompt_lengths[0]
    starts = jnp.cumsum(lengths) - lengths
    query_start = jnp.max(
        jnp.where(starts[None, :] <= query_pos[:, None], starts[None, :], 0), axis=1
    )
    allowed = (
        (key_pos[None, :] <= query_pos[:, None]) & (key_pos[None, :] >= query_start[:, None])
    ).astype(F32)
    scores = jnp.einsum("qhe,khe->hqk", query, pair[:, 0], preferred_element_type=F32)
    weights = softmax_weights(scores, allowed[None])
    text_heads = jnp.einsum("hqk,khe->qhe", weights, pair[:, 1], preferred_element_type=F32)
    text_heads = text_heads.astype(BF).reshape(piece_rows, half)
    partial = lax.dot_general(
        text_heads, full_d[:, 3 * half :], (((1,), (1,)), ((), ())), preferred_element_type=F32
    ).astype(BF)
    sub = lax.axis_index("sub")
    keep_rows = piece_rows // 2
    give = lax.dynamic_slice_in_dim(partial, (1 - sub) * keep_rows, keep_rows, 0)
    keep = lax.dynamic_slice_in_dim(partial, sub * keep_rows, keep_rows, 0)
    total = (keep.astype(F32) + swap_sub(give).astype(F32)).astype(BF)
    return lax.dot_general(
        total, reorder, (((1,), (1,)), ((), ())), preferred_element_type=F32
    ).astype(BF)


def solution(mesh):
    grp, tok, sub = mesh.devices.shape
    lined = Mesh(mesh.devices.reshape(grp, 4, 4, tok // 16, sub), ("grp", "y", "x", "zh", "sub"))
    whole = ("grp",) + TOK
    placed = (
        P(whole, None),
        P(whole, None),
        P(TOK, "sub", None, None),
        P("sub", TOK),
        P(TOK, "sub"),
        P(whole, None),
        P("grp", TOK),
        P("grp", None),
        P(whole, "sub", None, None),
        P("sub", whole),
    )
    return jax.shard_map(
        shards,
        mesh=lined,
        in_specs=placed,
        out_specs=P(whole + ("sub",), None),
        check_vma=False,
    )
```

```python
import math

import jax
import jax.numpy as jnp
from jax import lax
from jax.sharding import Mesh
from jax.sharding import PartitionSpec as P

HD = 88
REACH = 3
EPS = 1e-06
TOK = ("y", "x", "zh")
PLANE = ("y", "x")
BF = jnp.bfloat16
F32 = jnp.float32


def layer_norm(values):
    center = values - jnp.mean(values, axis=-1, keepdims=True)
    spread = jnp.mean(center * center, axis=-1, keepdims=True)
    return center * lax.rsqrt(spread + EPS)


def softmax_weights(scores, allowed):
    raw = jnp.exp(scores * (1.0 / math.sqrt(HD))) * allowed
    return (raw / jnp.sum(raw, axis=-1, keepdims=True)).astype(BF)


def swap_sub(value):
    return lax.ppermute(value, "sub", [(0, 1), (1, 0)])


def dot(a, b):
    return jnp.dot(a, b, preferred_element_type=F32)


def both_halves(part, first):
    other = swap_sub(part)
    return jnp.concatenate(
        [jnp.where(first, part, other), jnp.where(first, other, part)], axis=1
    )


def pad_to(columns):
    return -columns % 128


def to_all(value, axes):
    count = lax.axis_size(axes)
    spread = jnp.broadcast_to(value[None], (count,) + value.shape)
    return lax.all_to_all(spread, axes, split_axis=0, concat_axis=0, tiled=True)


def shards(
    patches,
    image_sizes,
    vision_inproj,
    vision_outproj,
    merger_weight,
    text_embed,
    image_positions,
    prompt_lengths,
    decoder_inproj,
    decoder_outproj,
):
    lines = lax.axis_size("zh")
    planes = lax.axis_size(PLANE)
    pieces = lax.axis_size(TOK)
    rows_v, width = patches.shape
    half = vision_inproj.shape[3]
    quarter = half // lines
    heads_line = quarter // HD
    krows = vision_inproj.shape[0]
    mrows = merger_weight.shape[0]

    vin = vision_inproj.reshape(krows, 3, lines, quarter).transpose(2, 0, 1, 3)
    vin = vin.reshape(lines, krows, 3 * quarter)
    vin = jnp.pad(vin, ((0, 0), (0, 0), (0, pad_to(3 * quarter))))
    vout = jnp.pad(vision_outproj.T, ((0, 0), (0, pad_to(half))))
    vout = jnp.broadcast_to(vout[None], (lines,) + vout.shape)
    line = jnp.concatenate([vin, vout], axis=2)
    line, decoder_inproj, decoder_outproj = lax.optimization_barrier(
        (line, decoder_inproj, decoder_outproj)
    )
    line = lax.all_to_all(line, "zh", split_axis=0, concat_axis=0, tiled=True)
    split_out = vin.shape[2]
    split_merge = line.shape[2]
    line_v = line.reshape(lines * krows, split_merge)
    merge = jnp.pad(merger_weight, ((0, 0), (0, pad_to(half))))
    line_v = jnp.concatenate([line_v, merge], axis=1)

    drows = decoder_inproj.shape[0]
    dec = jnp.concatenate(
        [decoder_inproj.reshape(drows, 3, half).transpose(1, 0, 2), decoder_outproj.T[None]], axis=0
    )
    dec_other = lax.ppermute(dec, "grp", [(0, 1), (1, 0)])
    low = lax.axis_index("grp") == 0
    dec = jnp.stack([jnp.where(low, dec, dec_other), jnp.where(low, dec_other, dec)], axis=1)
    dec = dec.reshape(8 * drows, half)
    patch_rows = patches.astype(F32)
    normed = layer_norm(patch_rows).astype(BF)
    line_v, dec, normed, text = lax.optimization_barrier((line_v, dec, normed, text_embed))
    full_v = lax.all_gather(line_v, PLANE, axis=0, tiled=True)
    line_d = to_all(dec, "zh").reshape(lines, 4, 2 * drows, half).transpose(0, 2, 1, 3)
    line_d = line_d.reshape(lines * 2 * drows, 4 * half)
    full_d = lax.all_gather(line_d, PLANE, axis=0, tiled=True)
    order = jnp.arange(width, dtype=jnp.int32)
    natural = (
        order // drows % 2 * (width // 2) + order // (2 * drows) * drows + order % drows
    )
    reorder = (natural[None, :] == order[:, None]).astype(BF)

    piece_rows = text_embed.shape[0]
    reach = REACH + 1
    cap = rows_v // (2 * pieces)
    slots = reach * cap
    targets = image_positions[0]
    target_piece = targets // piece_rows
    target_row = targets % piece_rows
    hits = (target_piece[:, None] == jnp.arange(pieces, dtype=jnp.int32)[None, :]).astype(jnp.int32)
    slot = jnp.sum((jnp.cumsum(hits, axis=0) - hits) * hits, axis=1)
    dest = jnp.arange(pieces * slots, dtype=jnp.int32)
    back = dest // cap % reach
    wanted = (dest // slots)[:, None] - back[:, None] == target_piece[None, :]
    wanted = wanted & ((dest % cap)[:, None] == slot[None, :])
    window_rows = reach * piece_rows

    first = lax.axis_index("sub") == 0
    ends = jnp.cumsum(image_sizes[0]).astype(BF)
    mark = jnp.zeros((16, width), BF).at[0, : ends.shape[0]].set(ends)
    side = rows_v // 2
    mine = jnp.concatenate([jnp.where(first, normed[:side], normed[side:]), mark], axis=0)
    moved = jnp.stack(
        [
            lax.ppermute(mine, "zh", [(i, (i + s) % lines) for i in range(lines)])
            for s in range(1, lines)
        ]
    )
    others = both_halves(moved[:, :side], first)
    others, reorder = lax.optimization_barrier((others, reorder))
    side_t = piece_rows // 2
    mine = jnp.where(first, text[:side_t], text[side_t:])
    earlier = jnp.stack(
        [
            lax.ppermute(mine, TOK, [(i, i + s) for i in range(pieces - s)])
            for s in range(REACH, 0, -1)
        ]
    )
    earlier = both_halves(earlier, first).reshape(REACH * piece_rows, width)
    window_text = jnp.concatenate([earlier, text], axis=0)

    normed = jnp.concatenate([normed[None], others]).reshape(lines * rows_v, width)
    ends_all = jnp.concatenate([ends[None], moved[:, side, : ends.shape[0]]]).astype(jnp.int32)
    group_ids = jnp.arange(rows_v, dtype=jnp.int32) // 4
    image_ids = jnp.sum(
        (group_ids[None, :, None] >= ends_all[:, None, :]).astype(jnp.int32), axis=2
    )
    same = (image_ids[:, :, None] == image_ids[:, None, :]).astype(F32)
    projected = dot(normed, full_v[:, : 3 * quarter]).astype(BF)
    triple = projected.reshape(lines, rows_v, 3, heads_line, HD)
    scores = jnp.einsum(
        "pqhe,pkhe->phqk", triple[:, :, 0], triple[:, :, 1], preferred_element_type=F32
    )
    weights = softmax_weights(scores, same[:, None])
    heads = jnp.einsum("phqk,pkhe->pqhe", weights, triple[:, :, 2], preferred_element_type=F32)
    heads = heads.astype(BF).reshape(lines, rows_v, quarter)
    me = lax.axis_index("zh")
    heads = jnp.roll(heads[::-1], me + 1, axis=0)
    heads, window_text = lax.optimization_barrier((heads, window_text))
    heads = lax.all_to_all(heads, "zh", split_axis=0, concat_axis=0, tiled=True)
    heads = heads.transpose(1, 0, 2).reshape(rows_v, half)
    w_out = full_v[:, split_out : split_out + half]
    partial = lax.dot_general(heads, w_out, (((1,), (1,)), ((), ())), preferred_element_type=F32)
    partial = partial.astype(BF)
    hidden = patch_rows + (partial.astype(F32) + swap_sub(partial).astype(F32))
    tokens = rows_v // 4
    merged = layer_norm(hidden).astype(BF).reshape(tokens, planes, lines, mrows)
    merged = merged.transpose(2, 0, 1, 3).reshape(lines, tokens, planes * mrows)
    merged = lax.all_to_all(merged, "zh", split_axis=0, concat_axis=0, tiled=True)
    partial = dot(merged.reshape(lines * tokens, planes * mrows), full_v[:, split_merge : split_merge + half])
    partial = partial.astype(BF).reshape(lines, tokens, half)
    partial = lax.all_to_all(partial, "zh", split_axis=0, concat_axis=0, tiled=True)
    embedded = jnp.sum(partial.astype(F32), axis=0).astype(BF)

    note = jnp.stack([target_row, jnp.ones_like(target_row)], axis=1).astype(BF)
    note = jnp.pad(note, ((0, 0), (0, pad_to(half) - 2)))
    sent = dot(wanted.astype(BF), jnp.concatenate([embedded, note], axis=1)).astype(BF)
    got = lax.all_to_all(
        sent.reshape(pieces, slots, half + pad_to(half)), TOK, split_axis=0, concat_axis=0, tiled=True
    ).reshape(pieces * slots, half + pad_to(half))
    note = got[:, half : half + 2].astype(jnp.int32)
    arrived = jnp.arange(pieces * slots, dtype=jnp.int32) // cap % reach
    arrived = jnp.where(note[:, 1] > 0, (REACH - arrived) * piece_rows + note[:, 0], window_rows)
    place = jnp.arange(window_rows, dtype=jnp.int32)[:, None] == arrived[None, :]
    got = got[:, :half]
    image_full = both_halves(got, first)
    placed = dot(place.astype(BF), image_full)
    filled = jnp.any(place, axis=1)
    decoder_input = jnp.where(filled[:, None], placed, window_text.astype(F32))
    normed_text = layer_norm(decoder_input).astype(BF)
    normed_text = dot(normed_text, reorder).astype(BF)
    head_local = half // HD
    query = dot(normed_text[REACH * piece_rows :], full_d[:, :half]).astype(BF)
    pair = dot(normed_text, full_d[:, half : 3 * half]).astype(BF)
    query = query.reshape(piece_rows, head_local, HD)
    pair = pair.reshape(window_rows, 2, head_local, HD)

    piece_id = lax.axis_index(TOK)
    query_pos = piece_id * piece_rows + jnp.arange(piece_rows, dtype=jnp.int32)
    key_pos = (piece_id - REACH) * piece_rows + jnp.arange(window_rows, dtype=jnp.int32)
    lengths = prompt_lengths[0]
    starts = jnp.cumsum(lengths) - lengths
    query_start = jnp.max(
        jnp.where(starts[None, :] <= query_pos[:, None], starts[None, :], 0), axis=1
    )
    allowed = (
        (key_pos[None, :] <= query_pos[:, None]) & (key_pos[None, :] >= query_start[:, None])
    ).astype(F32)
    scores = jnp.einsum("qhe,khe->hqk", query, pair[:, 0], preferred_element_type=F32)
    weights = softmax_weights(scores, allowed[None])
    text_heads = jnp.einsum("hqk,khe->qhe", weights, pair[:, 1], preferred_element_type=F32)
    text_heads = text_heads.astype(BF).reshape(piece_rows, half)
    partial = lax.dot_general(
        text_heads, full_d[:, 3 * half :], (((1,), (1,)), ((), ())), preferred_element_type=F32
    ).astype(BF)
    sub = lax.axis_index("sub")
    keep_rows = piece_rows // 2
    give = lax.dynamic_slice_in_dim(partial, (1 - sub) * keep_rows, keep_rows, 0)
    keep = lax.dynamic_slice_in_dim(partial, sub * keep_rows, keep_rows, 0)
    total = (keep.astype(F32) + swap_sub(give).astype(F32)).astype(BF)
    return lax.dot_general(
        total, reorder, (((1,), (1,)), ((), ())), preferred_element_type=F32
    ).astype(BF)


def solution(mesh):
    grp, tok, sub = mesh.devices.shape
    lined = Mesh(mesh.devices.reshape(grp, 4, 4, tok // 16, sub), ("grp", "y", "x", "zh", "sub"))
    whole = ("grp",) + TOK
    placed = (
        P(whole, None),
        P(whole, None),
        P(TOK, "sub", None, None),
        P("sub", TOK),
        P(TOK, "sub"),
        P(whole, None),
        P("grp", TOK),
        P("grp", None),
        P(whole, "sub", None, None),
        P("sub", whole),
    )
    return jax.shard_map(
        shards,
        mesh=lined,
        in_specs=placed,
        out_specs=P(whole + ("sub",), None),
        check_vma=False,
    )
```

```python
import functools
import math

import jax
import jax.numpy as jnp
from jax import lax
from jax.experimental import pallas as pl
from jax.experimental.pallas import tpu as pltpu
from jax.sharding import Mesh
from jax.sharding import PartitionSpec as P

HD = 88
REACH = 3
EPS = 1e-06
TOK = ("y", "x", "zh")
PLANE = ("y", "x")
BF = jnp.bfloat16
F32 = jnp.float32


def layer_norm(values):
    center = values - jnp.mean(values, axis=-1, keepdims=True)
    spread = jnp.mean(center * center, axis=-1, keepdims=True)
    return center * lax.rsqrt(spread + EPS)


def softmax_weights(scores, allowed):
    raw = jnp.exp(scores * (1.0 / math.sqrt(HD))) * allowed
    return (raw / jnp.sum(raw, axis=-1, keepdims=True)).astype(BF)


def swap_sub(value):
    return lax.ppermute(value, "sub", [(0, 1), (1, 0)])


def dot(a, b):
    return jnp.dot(a, b, preferred_element_type=F32)


def both_halves(part, first):
    return join_halves(part, swap_sub(part), first)


def join_halves(part, other, first):
    return jnp.concatenate(
        [jnp.where(first, part, other), jnp.where(first, other, part)], axis=1
    )


def pad_to(columns):
    return -columns % 128


def to_all(value, axes):
    count = lax.axis_size(axes)
    spread = jnp.broadcast_to(value[None], (count,) + value.shape)
    return lax.all_to_all(spread, axes, split_axis=0, concat_axis=0, tiled=True)


def contract_last(a, b):
    return lax.dot_general(a, b, (((1,), (1,)), ((), ())), preferred_element_type=F32)


def contract_first(a, b):
    return lax.dot_general(a, b, (((0,), (0,)), ((), ())), preferred_element_type=F32)


def decoder_block(
    half, cap, info, got, other, text, reorder, weights_hbm, out, weights, heads, sem
):
    load = pltpu.make_async_copy(weights_hbm, weights, sem)
    load.start()
    sub = info[0]
    piece = info[1]
    rows = text.shape[0]
    block = rows // (REACH + 1)
    tokens = got.shape[0]

    note = got[:, half - half % 128 :].astype(F32)
    spare = half % 128
    row = note[:, spare : spare + 1].astype(jnp.int32)
    flag = note[:, spare + 1 : spare + 2]
    index = lax.broadcasted_iota(jnp.int32, (tokens, 1), 0)
    back = lax.rem(lax.div(index, cap), REACH + 1)
    target = jnp.where(flag > 0.5, (REACH - back) * block + row, rows)
    place = lax.broadcasted_iota(jnp.int32, (tokens, rows), 1) == target
    place = jnp.where(place, 1.0, 0.0).astype(BF)
    mine = reorder[pl.ds(pl.multiple_of(sub * half, 16), half), :]
    theirs = reorder[pl.ds(pl.multiple_of((1 - sub) * half, 16), half), :]
    image = dot(got[:, :half], mine) + dot(other[:, :half], theirs)
    placed = contract_first(place, image.astype(BF))
    filled = contract_first(place, jnp.ones((tokens, 128), BF))
    values = jnp.where(filled[:, :1] > 0.5, placed, text[...].astype(F32))
    normed = layer_norm(values).astype(BF)

    load.wait()
    query_pos = piece * block + lax.broadcasted_iota(jnp.int32, (block, 1), 0)
    key_pos = (piece - REACH) * block + lax.broadcasted_iota(jnp.int32, (1, rows), 1)
    start = jnp.zeros((block, 1), jnp.int32)
    for prompt in range(2, info.shape[0]):
        start = jnp.where(query_pos >= info[prompt], jnp.maximum(start, info[prompt]), start)
    allowed = jnp.where((key_pos <= query_pos) & (key_pos >= start), 1.0, 0.0)
    partial = attention(half, normed[REACH * block :], normed, weights, heads, allowed, None)
    out[...] = contract_last(partial, reorder[...]).astype(BF)


def attention(half, asking, asked, weights, heads, allowed, late):
    spare = half % 128
    span = half + spare
    query = dot(asking, weights[:, :span])
    key = dot(asked, weights[:, half - spare : 2 * half])
    if late is not None:
        late.wait()
    value = dot(asked, weights[:, 2 * half : 2 * half + span])
    heads[:, :spare] = jnp.zeros((asking.shape[0], spare), F32)
    for head in range(half // HD):
        at = head * HD
        score = contract_last(
            query[:, at : at + HD].astype(BF), key[:, spare + at : spare + at + HD].astype(BF)
        )
        raw = jnp.exp(score * (1.0 / math.sqrt(HD))) * allowed
        share = (raw * (1.0 / jnp.sum(raw, axis=1, keepdims=True))).astype(BF)
        heads[:, spare + at : spare + at + HD] = dot(share, value[:, at : at + HD].astype(BF))
    return contract_last(heads[...].astype(BF), weights[:, 3 * half - spare : 4 * half]).astype(BF)


def vision_block(half, ends, normed, weights_hbm, out, weights, heads, sems):
    early = pltpu.make_async_copy(
        weights_hbm.at[:, : 2 * half], weights.at[:, : 2 * half], sems.at[0]
    )
    late = pltpu.make_async_copy(
        weights_hbm.at[:, 2 * half : 4 * half], weights.at[:, 2 * half :], sems.at[1]
    )
    early.start()
    late.start()
    rows = normed.shape[0]

    def image_of(row):
        token = lax.shift_right_logical(row, 2)
        image = jnp.zeros(row.shape, jnp.int32)
        for step in range(ends.shape[0]):
            image = image + jnp.where(token >= ends[step], 1, 0)
        return image

    own = image_of(lax.broadcasted_iota(jnp.int32, (rows, 1), 0))
    seen = image_of(lax.broadcasted_iota(jnp.int32, (1, rows), 1))
    allowed = jnp.where(own == seen, 1.0, 0.0)
    patches = normed[...]
    early.wait()
    out[...] = attention(half, patches, patches, weights, heads, allowed, late)


def run_vision_block(half, ends, normed, weights):
    rows, width = normed.shape
    vmem = pl.BlockSpec(memory_space=pltpu.VMEM)
    return pl.pallas_call(
        functools.partial(vision_block, half),
        out_shape=jax.ShapeDtypeStruct((rows, width), BF),
        in_specs=[
            pl.BlockSpec(memory_space=pltpu.SMEM),
            vmem,
            pl.BlockSpec(memory_space=pl.ANY),
        ],
        out_specs=vmem,
        scratch_shapes=[
            pltpu.VMEM((width, 4 * half), BF),
            pltpu.VMEM((rows, half + half % 128), F32),
            pltpu.SemaphoreType.DMA((2,)),
        ],
        compiler_params=pltpu.CompilerParams(vmem_limit_bytes=56 << 20),
    )(ends, normed, weights)


def run_decoder_block(half, cap, info, got, other, text, reorder, weights):
    rows, width = text.shape
    block = rows // (REACH + 1)
    vmem = pl.BlockSpec(memory_space=pltpu.VMEM)
    return pl.pallas_call(
        functools.partial(decoder_block, half, cap),
        out_shape=jax.ShapeDtypeStruct((block, width), BF),
        in_specs=[pl.BlockSpec(memory_space=pltpu.SMEM)]
        + [vmem] * 4
        + [pl.BlockSpec(memory_space=pl.ANY)],
        out_specs=vmem,
        scratch_shapes=[
            pltpu.VMEM(weights.shape, BF),
            pltpu.VMEM((block, half + half % 128), F32),
            pltpu.SemaphoreType.DMA,
        ],
        compiler_params=pltpu.CompilerParams(vmem_limit_bytes=56 << 20),
    )(info, got, other, text, reorder, weights)


def shards(
    patches,
    image_sizes,
    vision_inproj,
    vision_outproj,
    merger_weight,
    text_embed,
    image_positions,
    prompt_lengths,
    decoder_inproj,
    decoder_outproj,
):
    lines = lax.axis_size("zh")
    planes = lax.axis_size(PLANE)
    pieces = lax.axis_size(TOK)
    rows_v, width = patches.shape
    half = vision_inproj.shape[3]
    krows = vision_inproj.shape[0]
    mrows = merger_weight.shape[0]

    line = jnp.concatenate(
        [vision_inproj.reshape(krows, 3 * half), vision_outproj.T], axis=1
    )
    line = to_all(line, "zh").reshape(lines * krows, 4 * half)
    merge = jnp.pad(merger_weight, ((0, 0), (0, pad_to(half))))
    line_v = jnp.concatenate([line, merge], axis=1)

    drows = decoder_inproj.shape[0]
    dec = decoder_inproj.reshape(drows, 3 * half)
    dec = jnp.stack(
        [
            dec[:, : 2 * half],
            jnp.concatenate([dec[:, 2 * half :], decoder_outproj.T], axis=1),
        ]
    )
    dec_other = lax.ppermute(dec, "grp", [(0, 1), (1, 0)])
    low = lax.axis_index("grp") == 0
    dec = jnp.stack([jnp.where(low, dec, dec_other), jnp.where(low, dec_other, dec)], axis=1)
    dec = dec.reshape(4 * drows, width)
    patch_rows = patches.astype(F32)
    normed = layer_norm(patch_rows).astype(BF)
    me = lax.axis_index("zh")
    order = jnp.arange(width, dtype=jnp.int32)
    fan = 2 * drows
    natural = (
        order // drows % 2 * (width // 2)
        + order // (lines * fan) * (lines * drows)
        + (me - order // fan) % lines * drows
        + order % drows
    )
    reorder = (natural[None, :] == order[:, None]).astype(BF)
    first = lax.axis_index("sub") == 0
    side_t = text_embed.shape[0] // 2
    mine = jnp.concatenate(
        [
            jnp.where(first, text_embed[:side_t], text_embed[side_t:]),
            dec,
            jnp.zeros((-4 * drows % 16, width), BF),
        ],
        axis=0,
    )
    line_v, normed, reorder, mine = lax.optimization_barrier((line_v, normed, reorder, mine))
    full_v = lax.all_gather(line_v, PLANE, axis=0, tiled=True)

    piece_rows = text_embed.shape[0]
    reach = REACH + 1
    cap = rows_v // (2 * pieces)
    slots = reach * cap
    targets = image_positions[0]
    target_piece = targets // piece_rows
    target_row = targets % piece_rows
    hits = (target_piece[:, None] == jnp.arange(pieces, dtype=jnp.int32)[None, :]).astype(jnp.int32)
    slot = jnp.sum((jnp.cumsum(hits, axis=0) - hits) * hits, axis=1)
    dest = jnp.arange(pieces * slots, dtype=jnp.int32)
    back = dest // cap % reach
    wanted = (dest // slots)[:, None] - back[:, None] == target_piece[None, :]
    wanted = wanted & ((dest % cap)[:, None] == slot[None, :])
    window_rows = reach * piece_rows

    moved = [
        lax.ppermute(mine, "zh", [(i, (i + s) % lines) for i in range(lines)])
        for s in range(1, lines)
    ]
    line_d = jnp.stack([m[side_t : side_t + 4 * drows] for m in [mine] + moved])
    line_d = jnp.concatenate([line_d[:, : 2 * drows], line_d[:, 2 * drows :]], axis=2)
    full_d = lax.all_gather(
        line_d.reshape(lines * 2 * drows, 4 * half), PLANE, axis=0, tiled=True
    )

    text = jnp.stack([m[:side_t] for m in moved[::-1]])
    before = lax.ppermute(text, PLANE, [(i, i + 1) for i in range(planes - 1)])
    steps = jnp.arange(REACH, 0, -1, dtype=jnp.int32)[:, None, None]
    text = both_halves(jnp.where(steps <= me, text, before), first)
    window_text = jnp.concatenate([text.reshape(REACH * piece_rows, width), text_embed], axis=0)
    window_text = dot(window_text, reorder).astype(BF)

    ends = jnp.cumsum(image_sizes[0])
    partial = run_vision_block(half, ends, normed, full_v)
    hidden = patch_rows + (partial.astype(F32) + swap_sub(partial).astype(F32))
    tokens = rows_v // 4
    merged = layer_norm(hidden).astype(BF).reshape(tokens, planes, lines, mrows)
    merged = merged.transpose(2, 0, 1, 3).reshape(lines, tokens, planes * mrows)
    merged = lax.all_to_all(merged, "zh", split_axis=0, concat_axis=0, tiled=True)
    partial = dot(merged.reshape(lines * tokens, planes * mrows), full_v[:, 4 * half : 5 * half])
    partial = partial.astype(BF).reshape(lines, tokens, half)
    partial = lax.all_to_all(partial, "zh", split_axis=0, concat_axis=0, tiled=True)
    embedded = jnp.sum(partial.astype(F32), axis=0).astype(BF)

    note = jnp.stack([target_row, jnp.ones_like(target_row)], axis=1).astype(BF)
    note = jnp.pad(note, ((0, 0), (0, pad_to(half) - 2)))
    sent = dot(wanted.astype(BF), jnp.concatenate([embedded, note], axis=1)).astype(BF)
    got = lax.all_to_all(
        sent.reshape(pieces, slots, half + pad_to(half)), TOK, split_axis=0, concat_axis=0, tiled=True
    ).reshape(pieces * slots, half + pad_to(half))
    got, window_text = lax.optimization_barrier((got, window_text))
    lengths = prompt_lengths[0]
    starts = jnp.cumsum(lengths) - lengths
    info = jnp.concatenate(
        [jnp.stack([lax.axis_index("sub"), lax.axis_index(TOK)]).astype(jnp.int32), starts]
    )
    partial = run_decoder_block(
        half, cap, info, got, swap_sub(got), window_text, reorder, full_d
    )
    sub = lax.axis_index("sub")
    keep_rows = piece_rows // 2
    give = lax.dynamic_slice_in_dim(partial, (1 - sub) * keep_rows, keep_rows, 0)
    keep = lax.dynamic_slice_in_dim(partial, sub * keep_rows, keep_rows, 0)
    return (keep.astype(F32) + swap_sub(give).astype(F32)).astype(BF)


def solution(mesh):
    grp, tok, sub = mesh.devices.shape
    lined = Mesh(mesh.devices.reshape(grp, 4, 4, tok // 16, sub), ("grp", "y", "x", "zh", "sub"))
    whole = ("grp",) + TOK
    placed = (
        P(whole, None),
        P(whole, None),
        P(TOK, "sub", None, None),
        P("sub", TOK),
        P(TOK, "sub"),
        P(whole, None),
        P("grp", TOK),
        P("grp", None),
        P(whole, "sub", None, None),
        P("sub", whole),
    )
    return jax.shard_map(
        shards,
        mesh=lined,
        in_specs=placed,
        out_specs=P(whole + ("sub",), None),
        check_vma=False,
    )
```

```python
import functools
import math

import jax
import jax.numpy as jnp
from jax import lax
from jax.experimental import pallas as pl
from jax.experimental.pallas import tpu as pltpu
from jax.sharding import Mesh
from jax.sharding import PartitionSpec as P

HD = 88
REACH = 3
EPS = 1e-06
TOK = ("y", "x", "zh")
PLANE = ("y", "x")
BF = jnp.bfloat16
F32 = jnp.float32


def layer_norm(values):
    center = values - jnp.mean(values, axis=-1, keepdims=True)
    spread = jnp.mean(center * center, axis=-1, keepdims=True)
    return center * lax.rsqrt(spread + EPS)


def softmax_weights(scores, allowed):
    raw = jnp.exp(scores * (1.0 / math.sqrt(HD))) * allowed
    return (raw / jnp.sum(raw, axis=-1, keepdims=True)).astype(BF)


def swap_sub(value):
    return lax.ppermute(value, "sub", [(0, 1), (1, 0)])


def dot(a, b):
    return jnp.dot(a, b, preferred_element_type=F32)


def both_halves(part, first):
    return join_halves(part, swap_sub(part), first)


def join_halves(part, other, first):
    return jnp.concatenate(
        [jnp.where(first, part, other), jnp.where(first, other, part)], axis=1
    )


def pad_to(columns):
    return -columns % 128


def to_all(value, axes):
    count = lax.axis_size(axes)
    spread = jnp.broadcast_to(value[None], (count,) + value.shape)
    return lax.all_to_all(spread, axes, split_axis=0, concat_axis=0, tiled=True)


def contract_last(a, b):
    return lax.dot_general(a, b, (((1,), (1,)), ((), ())), preferred_element_type=F32)


def contract_first(a, b):
    return lax.dot_general(a, b, (((0,), (0,)), ((), ())), preferred_element_type=F32)


def decoder_block(
    half, cap, info, got, other, text, reorder, weights_hbm, keep, give, weights, heads, whole, sem
):
    load = pltpu.make_async_copy(weights_hbm, weights, sem)
    load.start()
    sub = info[0]
    piece = info[1]
    rows = text.shape[0]
    block = rows // (REACH + 1)
    tokens = got.shape[0]

    note = got[:, half - half % 128 :].astype(F32)
    spare = half % 128
    row = note[:, spare : spare + 1].astype(jnp.int32)
    flag = note[:, spare + 1 : spare + 2]
    index = lax.broadcasted_iota(jnp.int32, (tokens, 1), 0)
    back = lax.rem(lax.div(index, cap), REACH + 1)
    target = jnp.where(flag > 0.5, (REACH - back) * block + row, rows)
    place = lax.broadcasted_iota(jnp.int32, (tokens, rows), 1) == target
    place = jnp.where(place, 1.0, 0.0).astype(BF)
    mine = reorder[pl.ds(pl.multiple_of(sub * half, 16), half), :]
    theirs = reorder[pl.ds(pl.multiple_of((1 - sub) * half, 16), half), :]
    image = dot(got[:, :half], mine) + dot(other[:, :half], theirs)
    placed = contract_first(place, image.astype(BF))
    filled = contract_first(place, jnp.ones((tokens, 128), BF))
    values = jnp.where(filled[:, :1] > 0.5, placed, text[...].astype(F32))
    normed = layer_norm(values).astype(BF)

    load.wait()
    query_pos = piece * block + lax.broadcasted_iota(jnp.int32, (block, 1), 0)
    key_pos = (piece - REACH) * block + lax.broadcasted_iota(jnp.int32, (1, rows), 1)
    start = jnp.zeros((block, 1), jnp.int32)
    for prompt in range(2, info.shape[0]):
        start = jnp.where(query_pos >= info[prompt], jnp.maximum(start, info[prompt]), start)
    allowed = jnp.where((key_pos <= query_pos) & (key_pos >= start), 1.0, 0.0)
    partial = attention(half, normed[REACH * block :], normed, weights, heads, allowed, None)
    split_rows(contract_last(partial, reorder[...]).astype(BF), sub, keep, give, whole)


def attention(half, asking, asked, weights, heads, allowed, late):
    spare = half % 128
    span = half + spare
    query = dot(asking, weights[:, :span])
    key = dot(asked, weights[:, half - spare : 2 * half])
    if late is not None:
        late.wait()
    value = dot(asked, weights[:, 2 * half : 2 * half + span])
    heads[:, :spare] = jnp.zeros((asking.shape[0], spare), F32)
    for head in range(half // HD):
        at = head * HD
        score = contract_last(
            query[:, at : at + HD].astype(BF), key[:, spare + at : spare + at + HD].astype(BF)
        )
        raw = jnp.exp(score * (1.0 / math.sqrt(HD))) * allowed
        share = (raw * (1.0 / jnp.sum(raw, axis=1, keepdims=True))).astype(BF)
        heads[:, spare + at : spare + at + HD] = dot(share, value[:, at : at + HD].astype(BF))
    return contract_last(heads[...].astype(BF), weights[:, 3 * half - spare : 4 * half]).astype(BF)


def split_rows(values, sub, keep, give, whole):
    rows = keep.shape[0]
    whole[...] = values
    keep[...] = whole[pl.ds(pl.multiple_of(sub * rows, 16), rows), :]
    give[...] = whole[pl.ds(pl.multiple_of((1 - sub) * rows, 16), rows), :]


def vision_block(half, info, normed, weights_hbm, keep, give, weights, heads, whole, sems):
    early = pltpu.make_async_copy(
        weights_hbm.at[:, : 2 * half], weights.at[:, : 2 * half], sems.at[0]
    )
    late = pltpu.make_async_copy(
        weights_hbm.at[:, 2 * half : 4 * half], weights.at[:, 2 * half :], sems.at[1]
    )
    early.start()
    late.start()
    rows = normed.shape[0]

    def image_of(row):
        token = lax.rem(row, rows // 4)
        image = jnp.zeros(row.shape, jnp.int32)
        for step in range(1, info.shape[0]):
            image = image + jnp.where(token >= info[step], 1, 0)
        return image

    own = image_of(lax.broadcasted_iota(jnp.int32, (rows, 1), 0))
    seen = image_of(lax.broadcasted_iota(jnp.int32, (1, rows), 1))
    allowed = jnp.where(own == seen, 1.0, 0.0)
    patches = normed[...]
    early.wait()
    partial = attention(half, patches, patches, weights, heads, allowed, late)
    split_rows(partial, info[0], keep, give, whole)


def run_vision_block(half, info, normed, weights):
    rows, width = normed.shape
    vmem = pl.BlockSpec(memory_space=pltpu.VMEM)
    return pl.pallas_call(
        functools.partial(vision_block, half),
        out_shape=[jax.ShapeDtypeStruct((rows // 2, width), BF)] * 2,
        in_specs=[
            pl.BlockSpec(memory_space=pltpu.SMEM),
            vmem,
            pl.BlockSpec(memory_space=pl.ANY),
        ],
        out_specs=[vmem] * 2,
        scratch_shapes=[
            pltpu.VMEM((width, 4 * half), BF),
            pltpu.VMEM((rows, half + half % 128), F32),
            pltpu.VMEM((rows, width), BF),
            pltpu.SemaphoreType.DMA((2,)),
        ],
        compiler_params=pltpu.CompilerParams(vmem_limit_bytes=56 << 20),
    )(info, normed, weights)


def merger_rows(patches, keep, other, spread, out):
    hidden = patches[...].astype(F32) + (keep[...].astype(F32) + other[...].astype(F32))
    ready = dot(layer_norm(hidden).astype(BF), spread[...]).astype(BF)
    columns = out.shape[2]
    for place in range(out.shape[0]):
        out[place] = ready[:, place * columns : (place + 1) * columns]


def run_merger_rows(lines, patches, keep, other, spread):
    rows = patches.shape[0]
    vmem = pl.BlockSpec(memory_space=pltpu.VMEM)
    return pl.pallas_call(
        merger_rows,
        out_shape=jax.ShapeDtypeStruct((lines, rows, spread.shape[1] // lines), BF),
        in_specs=[vmem] * 4,
        out_specs=vmem,
        compiler_params=pltpu.CompilerParams(vmem_limit_bytes=56 << 20),
    )(patches, keep, other, spread)


def merger_dot(at, depth, info, mine, theirs, weights_hbm, out, weights, sem):
    load = pltpu.make_async_copy(weights_hbm.at[:, at : at + weights.shape[1]], weights, sem)
    load.start()
    sub = info[0]
    lines, rows = mine.shape[:2]
    half_rows = rows // 2
    load.wait()
    total = jnp.zeros((lines * half_rows, weights.shape[1]), F32)
    for side, values in ((sub, mine), (1 - sub, theirs)):
        for step in range(2):
            part = values[:, step * half_rows : (step + 1) * half_rows, :]
            part = part.reshape(lines * half_rows, part.shape[2])[:, :depth]
            row = pl.multiple_of((2 * side + step) * depth, 16)
            total = total + dot(part, weights[pl.ds(row, depth), :])
    out[...] = total[:, : out.shape[1]].astype(BF)


def run_merger_dot(half, depth, info, mine, theirs, weights):
    lines, rows = mine.shape[:2]
    vmem = pl.BlockSpec(memory_space=pltpu.VMEM)
    return pl.pallas_call(
        functools.partial(merger_dot, 4 * half, depth),
        out_shape=jax.ShapeDtypeStruct((lines * rows // 2, half), BF),
        in_specs=[pl.BlockSpec(memory_space=pltpu.SMEM), vmem, vmem]
        + [pl.BlockSpec(memory_space=pl.ANY)],
        out_specs=vmem,
        scratch_shapes=[
            pltpu.VMEM((weights.shape[0], weights.shape[1] - 4 * half), BF),
            pltpu.SemaphoreType.DMA,
        ],
        compiler_params=pltpu.CompilerParams(vmem_limit_bytes=56 << 20),
    )(info, mine, theirs, weights)


def run_decoder_block(half, cap, info, got, other, text, reorder, weights):
    rows, width = text.shape
    block = rows // (REACH + 1)
    vmem = pl.BlockSpec(memory_space=pltpu.VMEM)
    return pl.pallas_call(
        functools.partial(decoder_block, half, cap),
        out_shape=[jax.ShapeDtypeStruct((block // 2, width), BF)] * 2,
        in_specs=[pl.BlockSpec(memory_space=pltpu.SMEM)]
        + [vmem] * 4
        + [pl.BlockSpec(memory_space=pl.ANY)],
        out_specs=[vmem] * 2,
        scratch_shapes=[
            pltpu.VMEM(weights.shape, BF),
            pltpu.VMEM((block, half + half % 128), F32),
            pltpu.VMEM((block, width), BF),
            pltpu.SemaphoreType.DMA,
        ],
        compiler_params=pltpu.CompilerParams(vmem_limit_bytes=56 << 20),
    )(info, got, other, text, reorder, weights)


def shards(
    patches,
    image_sizes,
    vision_inproj,
    vision_outproj,
    merger_weight,
    text_embed,
    image_positions,
    prompt_lengths,
    decoder_inproj,
    decoder_outproj,
):
    lines = lax.axis_size("zh")
    planes = lax.axis_size(PLANE)
    pieces = lax.axis_size(TOK)
    rows_v, width = patches.shape
    half = vision_inproj.shape[3]
    krows = vision_inproj.shape[0]
    mrows = merger_weight.shape[0]

    line = jnp.concatenate(
        [vision_inproj.reshape(krows, 3 * half), vision_outproj.T], axis=1
    )
    line = to_all(line, "zh").reshape(lines * krows, 4 * half)
    merge = jnp.pad(merger_weight, ((0, 0), (0, pad_to(half))))
    line_v = jnp.concatenate([line, merge], axis=1)

    drows = decoder_inproj.shape[0]
    dec = decoder_inproj.reshape(drows, 3 * half)
    dec = jnp.stack(
        [
            dec[:, : 2 * half],
            jnp.concatenate([dec[:, 2 * half :], decoder_outproj.T], axis=1),
        ]
    )
    dec_other = lax.ppermute(dec, "grp", [(0, 1), (1, 0)])
    low = lax.axis_index("grp") == 0
    dec = jnp.stack([jnp.where(low, dec, dec_other), jnp.where(low, dec_other, dec)], axis=1)
    dec = dec.reshape(4 * drows, width)
    tokens = rows_v // 4
    patches = patches.reshape(tokens, 4, width).transpose(1, 0, 2).reshape(rows_v, width)
    sub = lax.axis_index("sub")
    side_v = rows_v // 2
    own_patches = jnp.where(sub == 0, patches[:side_v], patches[side_v:])
    normed = layer_norm(patches.astype(F32)).astype(BF)
    depth = 4 * mrows
    spread_at = jnp.arange(lines * (depth + pad_to(depth)), dtype=jnp.int32)
    inner = spread_at % (depth + pad_to(depth))
    source = inner // mrows * (lines * mrows) + inner % mrows
    source = source + spread_at // (depth + pad_to(depth)) * mrows
    source = jnp.where(inner < depth, source, width)
    spread = (jnp.arange(width, dtype=jnp.int32)[:, None] == source[None, :]).astype(BF)
    me = lax.axis_index("zh")
    order = jnp.arange(width, dtype=jnp.int32)
    fan = 2 * drows
    natural = (
        order // drows % 2 * (width // 2)
        + order // (lines * fan) * (lines * drows)
        + (me - order // fan) % lines * drows
        + order % drows
    )
    reorder = (natural[None, :] == order[:, None]).astype(BF)
    first = lax.axis_index("sub") == 0
    side_t = text_embed.shape[0] // 2
    mine = jnp.concatenate(
        [
            jnp.where(first, text_embed[:side_t], text_embed[side_t:]),
            dec,
            jnp.zeros((-4 * drows % 16, width), BF),
        ],
        axis=0,
    )
    line_v, normed, reorder, mine, spread, own_patches = lax.optimization_barrier(
        (line_v, normed, reorder, mine, spread, own_patches)
    )
    full_v = lax.all_gather(line_v, PLANE, axis=0, tiled=True)

    piece_rows = text_embed.shape[0]
    reach = REACH + 1
    cap = rows_v // (2 * pieces)
    slots = reach * cap
    targets = image_positions[0]
    target_piece = targets // piece_rows
    target_row = targets % piece_rows
    hits = (target_piece[:, None] == jnp.arange(pieces, dtype=jnp.int32)[None, :]).astype(jnp.int32)
    slot = jnp.sum((jnp.cumsum(hits, axis=0) - hits) * hits, axis=1)
    dest = jnp.arange(pieces * slots, dtype=jnp.int32)
    back = dest // cap % reach
    wanted = (dest // slots)[:, None] - back[:, None] == target_piece[None, :]
    wanted = wanted & ((dest % cap)[:, None] == slot[None, :])
    window_rows = reach * piece_rows

    moved = [
        lax.ppermute(mine, "zh", [(i, (i + s) % lines) for i in range(lines)])
        for s in range(1, lines)
    ]
    line_d = jnp.stack([m[side_t : side_t + 4 * drows] for m in [mine] + moved])
    line_d = jnp.concatenate([line_d[:, : 2 * drows], line_d[:, 2 * drows :]], axis=2)
    full_d = lax.all_gather(
        line_d.reshape(lines * 2 * drows, 4 * half), PLANE, axis=0, tiled=True
    )

    text = jnp.stack([m[:side_t] for m in moved[::-1]])
    before = lax.ppermute(text, PLANE, [(i, i + 1) for i in range(planes - 1)])
    steps = jnp.arange(REACH, 0, -1, dtype=jnp.int32)[:, None, None]
    text = both_halves(jnp.where(steps <= me, text, before), first)
    window_text = jnp.concatenate([text.reshape(REACH * piece_rows, width), text_embed], axis=0)
    window_text = dot(window_text, reorder).astype(BF)

    place_info = jnp.concatenate([sub.astype(jnp.int32)[None], jnp.cumsum(image_sizes[0])])
    keep, give = run_vision_block(half, place_info, normed, full_v)
    merged = run_merger_rows(lines, own_patches, keep, swap_sub(give), spread)
    merged = lax.all_to_all(merged, "zh", split_axis=0, concat_axis=0, tiled=True)
    partial = run_merger_dot(half, depth, place_info, merged, swap_sub(merged), full_v)
    partial = partial.reshape(lines, tokens, half)
    partial = lax.all_to_all(partial, "zh", split_axis=0, concat_axis=0, tiled=True)
    embedded = jnp.sum(partial.astype(F32), axis=0).astype(BF)

    note = jnp.stack([target_row, jnp.ones_like(target_row)], axis=1).astype(BF)
    note = jnp.pad(note, ((0, 0), (0, pad_to(half) - 2)))
    sent = dot(wanted.astype(BF), jnp.concatenate([embedded, note], axis=1)).astype(BF)
    got = lax.all_to_all(
        sent.reshape(pieces, slots, half + pad_to(half)), TOK, split_axis=0, concat_axis=0, tiled=True
    ).reshape(pieces * slots, half + pad_to(half))
    got, window_text = lax.optimization_barrier((got, window_text))
    lengths = prompt_lengths[0]
    starts = jnp.cumsum(lengths) - lengths
    info = jnp.concatenate(
        [jnp.stack([lax.axis_index("sub"), lax.axis_index(TOK)]).astype(jnp.int32), starts]
    )
    keep, give = run_decoder_block(
        half, cap, info, got, swap_sub(got), window_text, reorder, full_d
    )
    return (keep.astype(F32) + swap_sub(give).astype(F32)).astype(BF)


def solution(mesh):
    grp, tok, sub = mesh.devices.shape
    lined = Mesh(mesh.devices.reshape(grp, 4, 4, tok // 16, sub), ("grp", "y", "x", "zh", "sub"))
    whole = ("grp",) + TOK
    placed = (
        P(whole, None),
        P(whole, None),
        P(TOK, "sub", None, None),
        P("sub", TOK),
        P(TOK, "sub"),
        P(whole, None),
        P("grp", TOK),
        P("grp", None),
        P(whole, "sub", None, None),
        P("sub", whole),
    )
    return jax.shard_map(
        shards,
        mesh=lined,
        in_specs=placed,
        out_specs=P(whole + ("sub",), None),
        check_vma=False,
    )
```

```python
import functools
import math

import jax
import jax.numpy as jnp
from jax import lax
from jax.experimental import pallas as pl
from jax.experimental.pallas import tpu as pltpu
from jax.sharding import Mesh
from jax.sharding import PartitionSpec as P

HD = 88
REACH = 3
EPS = 1e-06
TOK = ("y", "x", "zh")
PLANE = ("y", "x")
BF = jnp.bfloat16
F32 = jnp.float32


def layer_norm(values):
    center = values - jnp.mean(values, axis=-1, keepdims=True)
    spread = jnp.mean(center * center, axis=-1, keepdims=True)
    return center * lax.rsqrt(spread + EPS)


def softmax_weights(scores, allowed):
    raw = jnp.exp(scores * (1.0 / math.sqrt(HD))) * allowed
    return (raw / jnp.sum(raw, axis=-1, keepdims=True)).astype(BF)


def swap_sub(value):
    return lax.ppermute(value, "sub", [(0, 1), (1, 0)])


def dot(a, b):
    return jnp.dot(a, b, preferred_element_type=F32)


def both_halves(part, first):
    return join_halves(part, swap_sub(part), first)


def join_halves(part, other, first):
    return jnp.concatenate(
        [jnp.where(first, part, other), jnp.where(first, other, part)], axis=1
    )


def pad_to(columns):
    return -columns % 128


def to_all(value, axes):
    count = lax.axis_size(axes)
    spread = jnp.broadcast_to(value[None], (count,) + value.shape)
    return lax.all_to_all(spread, axes, split_axis=0, concat_axis=0, tiled=True)


def contract_last(a, b):
    return lax.dot_general(a, b, (((1,), (1,)), ((), ())), preferred_element_type=F32)


def contract_first(a, b):
    return lax.dot_general(a, b, (((0,), (0,)), ((), ())), preferred_element_type=F32)


def decoder_block(
    half, cap, info, got, other, text, reorder, weights_hbm, keep, give, weights, heads, whole, sem
):
    load = pltpu.make_async_copy(weights_hbm, weights, sem)
    load.start()
    sub = info[0]
    piece = info[1]
    rows = text.shape[0]
    block = rows // (REACH + 1)
    tokens = got.shape[0]

    note = got[:, half - half % 128 :].astype(F32)
    spare = half % 128
    row = note[:, spare : spare + 1].astype(jnp.int32)
    flag = note[:, spare + 1 : spare + 2]
    index = lax.broadcasted_iota(jnp.int32, (tokens, 1), 0)
    back = lax.rem(lax.div(index, cap), REACH + 1)
    target = jnp.where(flag > 0.5, (REACH - back) * block + row, rows)
    place = lax.broadcasted_iota(jnp.int32, (tokens, rows), 1) == target
    place = jnp.where(place, 1.0, 0.0).astype(BF)
    mine = reorder[pl.ds(pl.multiple_of(sub * half, 16), half), :]
    theirs = reorder[pl.ds(pl.multiple_of((1 - sub) * half, 16), half), :]
    image = dot(got[:, :half], mine) + dot(other[:, :half], theirs)
    placed = contract_first(place, image.astype(BF))
    filled = contract_first(place, jnp.ones((tokens, 128), BF))
    values = jnp.where(filled[:, :1] > 0.5, placed, text[...].astype(F32))
    normed = layer_norm(values).astype(BF)

    load.wait()
    query_pos = piece * block + lax.broadcasted_iota(jnp.int32, (block, 1), 0)
    key_pos = (piece - REACH) * block + lax.broadcasted_iota(jnp.int32, (1, rows), 1)
    start = jnp.zeros((block, 1), jnp.int32)
    for prompt in range(2, info.shape[0]):
        start = jnp.where(query_pos >= info[prompt], jnp.maximum(start, info[prompt]), start)
    allowed = jnp.where((key_pos <= query_pos) & (key_pos >= start), 1.0, 0.0)
    partial = attention(half, normed[REACH * block :], normed, weights, heads, allowed)
    split_rows(contract_last(partial, reorder[...]).astype(BF), sub, keep, give, whole)


def attention(half, asking, asked, weights, heads, allowed):
    spare = half % 128
    span = half + spare
    query = dot(asking, weights[:, :span])
    key = dot(asked, weights[:, half - spare : 2 * half])
    value = dot(asked, weights[:, 2 * half : 2 * half + span])
    heads[:, :spare] = jnp.zeros((asking.shape[0], spare), F32)
    for head in range(half // HD):
        at = head * HD
        score = contract_last(
            query[:, at : at + HD].astype(BF), key[:, spare + at : spare + at + HD].astype(BF)
        )
        raw = jnp.exp(score * (1.0 / math.sqrt(HD))) * allowed
        share = (raw * (1.0 / jnp.sum(raw, axis=1, keepdims=True))).astype(BF)
        heads[:, spare + at : spare + at + HD] = dot(share, value[:, at : at + HD].astype(BF))
    return contract_last(heads[...].astype(BF), weights[:, 3 * half - spare : 4 * half]).astype(BF)


def split_rows(values, sub, keep, give, whole):
    rows = keep.shape[0]
    whole[...] = values
    keep[...] = whole[pl.ds(pl.multiple_of(sub * rows, 16), rows), :]
    give[...] = whole[pl.ds(pl.multiple_of((1 - sub) * rows, 16), rows), :]


def vision_block(at, part, info, own, other, weights_hbm, own_out, other_out, weights, heads, sem):
    base = at - at % 128
    load = pltpu.make_async_copy(weights_hbm.at[:, base : base + weights.shape[1]], weights, sem)
    load.start()
    rows = own.shape[0]
    images = info.shape[0] // 2
    load.wait()
    for side, (values, out) in enumerate(((own, own_out), (other, other_out))):

        def image_of(row):
            token = lax.rem(row, rows // 4)
            image = jnp.zeros(row.shape, jnp.int32)
            for step in range(images):
                image = image + jnp.where(token >= info[side * images + step], 1, 0)
            return image

        asking = image_of(lax.broadcasted_iota(jnp.int32, (rows, 1), 0))
        asked = image_of(lax.broadcasted_iota(jnp.int32, (1, rows), 1))
        allowed = jnp.where(asking == asked, 1.0, 0.0)
        triple = []
        for member in range(3):
            begin = at - base + member * part
            end = begin + part
            low = begin - begin % 128
            high = end + -end % 128
            triple.append((dot(values[...], weights[:, low:high]), begin - low))
        heads[...] = jnp.zeros(heads.shape, F32)
        for head in range(part // HD):
            query, key, value = (
                array[:, shift + head * HD : shift + (head + 1) * HD].astype(BF)
                for array, shift in triple
            )
            raw = jnp.exp(contract_last(query, key) * (1.0 / math.sqrt(HD))) * allowed
            share = (raw * (1.0 / jnp.sum(raw, axis=1, keepdims=True))).astype(BF)
            heads[:, head * HD : (head + 1) * HD] = dot(share, value)
        out[...] = heads[...].astype(BF)


def run_vision_block(at, part, info, own, other, weights):
    rows, width = own.shape
    vmem = pl.BlockSpec(memory_space=pltpu.VMEM)
    end = at + 3 * part
    return pl.pallas_call(
        functools.partial(vision_block, at, part),
        out_shape=[jax.ShapeDtypeStruct((rows, part + pad_to(part)), BF)] * 2,
        in_specs=[pl.BlockSpec(memory_space=pltpu.SMEM), vmem, vmem]
        + [pl.BlockSpec(memory_space=pl.ANY)],
        out_specs=[vmem] * 2,
        scratch_shapes=[
            pltpu.VMEM((width, end + pad_to(end) - (at - at % 128)), BF),
            pltpu.VMEM((rows, part + pad_to(part)), F32),
            pltpu.SemaphoreType.DMA,
        ],
        compiler_params=pltpu.CompilerParams(vmem_limit_bytes=56 << 20),
    )(info, own, other, weights)


def vision_output(at, part, info, own, other, weights_hbm, keep, give, weights, heads, whole, sem):
    base = at - at % 128
    load = pltpu.make_async_copy(weights_hbm.at[:, base : base + weights.shape[1]], weights, sem)
    load.start()
    heads[...] = jnp.zeros(heads.shape, F32)
    low = info[1] == 0
    begin = at - base
    mine = own[...].astype(F32)[:, :part]
    theirs = other[...].astype(F32)[:, :part]
    heads[:, begin : begin + part] = jnp.where(low, mine, theirs)
    heads[:, begin + part : begin + 2 * part] = jnp.where(low, theirs, mine)
    load.wait()
    partial = contract_last(heads[...].astype(BF), weights[...])
    split_rows(partial.astype(BF), info[0], keep, give, whole)


def run_vision_output(at, part, info, own, other, weights):
    rows = own.shape[0]
    width = weights.shape[0]
    end = at + 2 * part
    span = end + pad_to(end) - (at - at % 128)
    vmem = pl.BlockSpec(memory_space=pltpu.VMEM)
    return pl.pallas_call(
        functools.partial(vision_output, at, part),
        out_shape=[jax.ShapeDtypeStruct((rows // 2, width), BF)] * 2,
        in_specs=[pl.BlockSpec(memory_space=pltpu.SMEM), vmem, vmem]
        + [pl.BlockSpec(memory_space=pl.ANY)],
        out_specs=[vmem] * 2,
        scratch_shapes=[
            pltpu.VMEM((width, span), BF),
            pltpu.VMEM((rows, span), F32),
            pltpu.VMEM((rows, width), BF),
            pltpu.SemaphoreType.DMA,
        ],
        compiler_params=pltpu.CompilerParams(vmem_limit_bytes=56 << 20),
    )(info, own, other, weights)


def merger_rows(patches, keep, other, spread, out):
    hidden = patches[...].astype(F32) + (keep[...].astype(F32) + other[...].astype(F32))
    ready = dot(layer_norm(hidden).astype(BF), spread[...]).astype(BF)
    columns = out.shape[2]
    for place in range(out.shape[0]):
        out[place] = ready[:, place * columns : (place + 1) * columns]


def run_merger_rows(lines, patches, keep, other, spread):
    rows = patches.shape[0]
    vmem = pl.BlockSpec(memory_space=pltpu.VMEM)
    return pl.pallas_call(
        merger_rows,
        out_shape=jax.ShapeDtypeStruct((lines, rows, spread.shape[1] // lines), BF),
        in_specs=[vmem] * 4,
        out_specs=vmem,
        compiler_params=pltpu.CompilerParams(vmem_limit_bytes=56 << 20),
    )(patches, keep, other, spread)


def merger_dot(depth, info, mine, theirs, weights_hbm, out, weights, sem):
    load = pltpu.make_async_copy(weights_hbm.at[:, : weights.shape[1]], weights, sem)
    load.start()
    sub = info[0]
    lines, rows = mine.shape[:2]
    half_rows = rows // 2
    load.wait()
    total = jnp.zeros((lines * half_rows, weights.shape[1]), F32)
    for side, values in ((sub, mine), (1 - sub, theirs)):
        for step in range(2):
            part = values[:, step * half_rows : (step + 1) * half_rows, :]
            part = part.reshape(lines * half_rows, part.shape[2])[:, :depth]
            row = pl.multiple_of((2 * side + step) * depth, 16)
            total = total + dot(part, weights[pl.ds(row, depth), :])
    out[...] = total[:, : out.shape[1]].astype(BF)


def run_merger_dot(half, depth, info, mine, theirs, weights):
    lines, rows = mine.shape[:2]
    vmem = pl.BlockSpec(memory_space=pltpu.VMEM)
    return pl.pallas_call(
        functools.partial(merger_dot, depth),
        out_shape=jax.ShapeDtypeStruct((lines * rows // 2, half), BF),
        in_specs=[pl.BlockSpec(memory_space=pltpu.SMEM), vmem, vmem]
        + [pl.BlockSpec(memory_space=pl.ANY)],
        out_specs=vmem,
        scratch_shapes=[
            pltpu.VMEM((weights.shape[0], half + pad_to(half)), BF),
            pltpu.SemaphoreType.DMA,
        ],
        compiler_params=pltpu.CompilerParams(vmem_limit_bytes=56 << 20),
    )(info, mine, theirs, weights)


def run_decoder_block(half, cap, info, got, other, text, reorder, weights):
    rows, width = text.shape
    block = rows // (REACH + 1)
    vmem = pl.BlockSpec(memory_space=pltpu.VMEM)
    return pl.pallas_call(
        functools.partial(decoder_block, half, cap),
        out_shape=[jax.ShapeDtypeStruct((block // 2, width), BF)] * 2,
        in_specs=[pl.BlockSpec(memory_space=pltpu.SMEM)]
        + [vmem] * 4
        + [pl.BlockSpec(memory_space=pl.ANY)],
        out_specs=[vmem] * 2,
        scratch_shapes=[
            pltpu.VMEM(weights.shape, BF),
            pltpu.VMEM((block, half + half % 128), F32),
            pltpu.VMEM((block, width), BF),
            pltpu.SemaphoreType.DMA,
        ],
        compiler_params=pltpu.CompilerParams(vmem_limit_bytes=56 << 20),
    )(info, got, other, text, reorder, weights)


def shards(
    patches,
    image_sizes,
    vision_inproj,
    vision_outproj,
    merger_weight,
    text_embed,
    image_positions,
    prompt_lengths,
    decoder_inproj,
    decoder_outproj,
):
    lines = lax.axis_size("zh")
    planes = lax.axis_size(PLANE)
    pieces = lax.axis_size(TOK)
    rows_v, width = patches.shape
    half = vision_inproj.shape[3]
    krows = vision_inproj.shape[0]
    mrows = merger_weight.shape[0]

    group = lax.axis_index("grp")
    part = half // 2
    vin = vision_inproj.reshape(krows, 3, 2, part)
    vin = jnp.where(group == 0, vin[:, :, 0], vin[:, :, 1]).reshape(krows, 3 * part)
    line = jnp.concatenate([vin, vision_outproj.T], axis=1)
    line = to_all(line, "zh").reshape(lines * krows, 3 * part + half)
    at_in = half + pad_to(half)
    at_out = at_in + 3 * part
    end = at_out + half
    merge = jnp.pad(merger_weight, ((0, 0), (0, pad_to(half))))
    line_v = jnp.concatenate([merge, line, jnp.zeros((mrows, pad_to(end)), BF)], axis=1)

    drows = decoder_inproj.shape[0]
    dec = decoder_inproj.reshape(drows, 3 * half)
    dec = jnp.stack(
        [
            dec[:, : 2 * half],
            jnp.concatenate([dec[:, 2 * half :], decoder_outproj.T], axis=1),
        ]
    )
    dec_other = lax.ppermute(dec, "grp", [(0, 1), (1, 0)])
    low = lax.axis_index("grp") == 0
    dec = jnp.stack([jnp.where(low, dec, dec_other), jnp.where(low, dec_other, dec)], axis=1)
    dec = dec.reshape(4 * drows, width)
    tokens = rows_v // 4
    patches = patches.reshape(tokens, 4, width).transpose(1, 0, 2).reshape(rows_v, width)
    sub = lax.axis_index("sub")
    side_v = rows_v // 2
    own_patches = jnp.where(sub == 0, patches[:side_v], patches[side_v:])
    normed = layer_norm(patches.astype(F32)).astype(BF)
    ends = jnp.cumsum(image_sizes[0])
    mark = jnp.pad(ends.astype(BF)[None], ((0, 15), (0, width - ends.shape[0])))
    marked = jnp.concatenate([normed, mark], axis=0)
    depth = 4 * mrows
    spread_at = jnp.arange(lines * (depth + pad_to(depth)), dtype=jnp.int32)
    inner = spread_at % (depth + pad_to(depth))
    source = inner // mrows * (lines * mrows) + inner % mrows
    source = source + spread_at // (depth + pad_to(depth)) * mrows
    source = jnp.where(inner < depth, source, width)
    spread = (jnp.arange(width, dtype=jnp.int32)[:, None] == source[None, :]).astype(BF)
    me = lax.axis_index("zh")
    order = jnp.arange(width, dtype=jnp.int32)
    fan = 2 * drows
    natural = (
        order // drows % 2 * (width // 2)
        + order // (lines * fan) * (lines * drows)
        + (me - order // fan) % lines * drows
        + order % drows
    )
    reorder = (natural[None, :] == order[:, None]).astype(BF)
    first = lax.axis_index("sub") == 0
    side_t = text_embed.shape[0] // 2
    mine = jnp.concatenate(
        [
            jnp.where(first, text_embed[:side_t], text_embed[side_t:]),
            dec,
            jnp.zeros((-4 * drows % 16, width), BF),
        ],
        axis=0,
    )
    line_v, marked, reorder, mine, spread, own_patches = lax.optimization_barrier(
        (line_v, marked, reorder, mine, spread, own_patches)
    )
    full_v = lax.all_gather(line_v, PLANE, axis=0, tiled=True)

    piece_rows = text_embed.shape[0]
    reach = REACH + 1
    cap = rows_v // (2 * pieces)
    slots = reach * cap
    targets = image_positions[0]
    target_piece = targets // piece_rows
    target_row = targets % piece_rows
    hits = (target_piece[:, None] == jnp.arange(pieces, dtype=jnp.int32)[None, :]).astype(jnp.int32)
    slot = jnp.sum((jnp.cumsum(hits, axis=0) - hits) * hits, axis=1)
    dest = jnp.arange(pieces * slots, dtype=jnp.int32)
    back = dest // cap % reach
    wanted = (dest // slots)[:, None] - back[:, None] == target_piece[None, :]
    wanted = wanted & ((dest % cap)[:, None] == slot[None, :])
    window_rows = reach * piece_rows

    moved = [
        lax.ppermute(mine, "zh", [(i, (i + s) % lines) for i in range(lines)])
        for s in range(1, lines)
    ]
    line_d = jnp.stack([m[side_t : side_t + 4 * drows] for m in [mine] + moved])
    line_d = jnp.concatenate([line_d[:, : 2 * drows], line_d[:, 2 * drows :]], axis=2)
    full_d = lax.all_gather(
        line_d.reshape(lines * 2 * drows, 4 * half), PLANE, axis=0, tiled=True
    )

    text = jnp.stack([m[:side_t] for m in moved[::-1]])
    before = lax.ppermute(text, PLANE, [(i, i + 1) for i in range(planes - 1)])
    steps = jnp.arange(REACH, 0, -1, dtype=jnp.int32)[:, None, None]
    text = both_halves(jnp.where(steps <= me, text, before), first)
    window_text = jnp.concatenate([text.reshape(REACH * piece_rows, width), text_embed], axis=0)
    window_text = dot(window_text, reorder).astype(BF)

    place_info = jnp.stack([sub, group]).astype(jnp.int32)
    pair = [(0, 1), (1, 0)]
    paired = lax.ppermute(marked, "grp", pair)
    both_ends = jnp.concatenate([ends, paired[rows_v, : ends.shape[0]].astype(jnp.int32)])
    heads, heads_away = run_vision_block(
        at_in, part, both_ends, marked[:rows_v], paired[:rows_v], full_v
    )
    heads_back = lax.ppermute(heads_away, "grp", pair)
    keep, give = run_vision_output(at_out, part, place_info, heads, heads_back, full_v)
    merged = run_merger_rows(lines, own_patches, keep, swap_sub(give), spread)
    merged = lax.all_to_all(merged, "zh", split_axis=0, concat_axis=0, tiled=True)
    partial = run_merger_dot(half, depth, place_info, merged, swap_sub(merged), full_v)
    partial = partial.reshape(lines, tokens, half)
    partial = lax.all_to_all(partial, "zh", split_axis=0, concat_axis=0, tiled=True)
    embedded = jnp.sum(partial.astype(F32), axis=0).astype(BF)

    note = jnp.stack([target_row, jnp.ones_like(target_row)], axis=1).astype(BF)
    note = jnp.pad(note, ((0, 0), (0, pad_to(half) - 2)))
    sent = dot(wanted.astype(BF), jnp.concatenate([embedded, note], axis=1)).astype(BF)
    got = lax.all_to_all(
        sent.reshape(pieces, slots, half + pad_to(half)), TOK, split_axis=0, concat_axis=0, tiled=True
    ).reshape(pieces * slots, half + pad_to(half))
    got, window_text = lax.optimization_barrier((got, window_text))
    lengths = prompt_lengths[0]
    starts = jnp.cumsum(lengths) - lengths
    info = jnp.concatenate(
        [jnp.stack([lax.axis_index("sub"), lax.axis_index(TOK)]).astype(jnp.int32), starts]
    )
    keep, give = run_decoder_block(
        half, cap, info, got, swap_sub(got), window_text, reorder, full_d
    )
    return (keep.astype(F32) + swap_sub(give).astype(F32)).astype(BF)


def solution(mesh):
    grp, tok, sub = mesh.devices.shape
    lined = Mesh(mesh.devices.reshape(grp, 4, 4, tok // 16, sub), ("grp", "y", "x", "zh", "sub"))
    whole = ("grp",) + TOK
    placed = (
        P(whole, None),
        P(whole, None),
        P(TOK, "sub", None, None),
        P("sub", TOK),
        P(TOK, "sub"),
        P(whole, None),
        P("grp", TOK),
        P("grp", None),
        P(whole, "sub", None, None),
        P("sub", whole),
    )
    return jax.shard_map(
        shards,
        mesh=lined,
        in_specs=placed,
        out_specs=P(whole + ("sub",), None),
        check_vma=False,
    )
```

```python
import functools
import math

import jax
import jax.numpy as jnp
from jax import lax
from jax.experimental import pallas as pl
from jax.experimental.pallas import tpu as pltpu
from jax.sharding import Mesh
from jax.sharding import PartitionSpec as P

HD = 88
REACH = 3
EPS = 1e-06
TOK = ("y", "x", "zh")
PLANE = ("y", "x")
BF = jnp.bfloat16
F32 = jnp.float32


def layer_norm(values):
    center = values - jnp.mean(values, axis=-1, keepdims=True)
    spread = jnp.mean(center * center, axis=-1, keepdims=True)
    return center * lax.rsqrt(spread + EPS)


def softmax_weights(scores, allowed):
    raw = jnp.exp(scores * (1.0 / math.sqrt(HD))) * allowed
    return (raw / jnp.sum(raw, axis=-1, keepdims=True)).astype(BF)


def swap_sub(value):
    return lax.ppermute(value, "sub", [(0, 1), (1, 0)])


def dot(a, b):
    return jnp.dot(a, b, preferred_element_type=F32)


def both_halves(part, first):
    return join_halves(part, swap_sub(part), first)


def join_halves(part, other, first):
    return jnp.concatenate(
        [jnp.where(first, part, other), jnp.where(first, other, part)], axis=1
    )


def pad_to(columns):
    return -columns % 128


def to_all(value, axes):
    count = lax.axis_size(axes)
    spread = jnp.broadcast_to(value[None], (count,) + value.shape)
    return lax.all_to_all(spread, axes, split_axis=0, concat_axis=0, tiled=True)


def contract_last(a, b):
    return lax.dot_general(a, b, (((1,), (1,)), ((), ())), preferred_element_type=F32)


def contract_first(a, b):
    return lax.dot_general(a, b, (((0,), (0,)), ((), ())), preferred_element_type=F32)


def decoder_block(
    half, cap, info, got, other, text, reorder, weights_hbm, keep, give, weights, heads, whole, sem
):
    load = pltpu.make_async_copy(weights_hbm, weights, sem)
    load.start()
    sub = info[0]
    piece = info[1]
    rows = text.shape[0]
    block = rows // (REACH + 1)
    tokens = got.shape[0]

    note = got[:, half - half % 128 :].astype(F32)
    spare = half % 128
    row = note[:, spare : spare + 1].astype(jnp.int32)
    flag = note[:, spare + 1 : spare + 2]
    index = lax.broadcasted_iota(jnp.int32, (tokens, 1), 0)
    back = lax.rem(lax.div(index, cap), REACH + 1)
    target = jnp.where(flag > 0.5, (REACH - back) * block + row, rows)
    place = lax.broadcasted_iota(jnp.int32, (tokens, rows), 1) == target
    place = jnp.where(place, 1.0, 0.0).astype(BF)
    mine = reorder[pl.ds(pl.multiple_of(sub * half, 16), half), :]
    theirs = reorder[pl.ds(pl.multiple_of((1 - sub) * half, 16), half), :]
    image = dot(got[:, :half], mine) + dot(other[:, :half], theirs)
    placed = contract_first(place, image.astype(BF))
    filled = contract_first(place, jnp.ones((tokens, 128), BF))
    values = jnp.where(filled[:, :1] > 0.5, placed, text[...].astype(F32))
    normed = layer_norm(values).astype(BF)

    load.wait()
    query_pos = piece * block + lax.broadcasted_iota(jnp.int32, (block, 1), 0)
    key_pos = (piece - REACH) * block + lax.broadcasted_iota(jnp.int32, (1, rows), 1)
    start = jnp.zeros((block, 1), jnp.int32)
    for prompt in range(2, info.shape[0]):
        start = jnp.where(query_pos >= info[prompt], jnp.maximum(start, info[prompt]), start)
    allowed = jnp.where((key_pos <= query_pos) & (key_pos >= start), 1.0, 0.0)
    partial = attention(half, normed[REACH * block :], normed, weights, heads, allowed)
    split_rows(contract_last(partial, reorder[...]).astype(BF), sub, keep, give, whole)


def attention(half, asking, asked, weights, heads, allowed):
    spare = half % 128
    span = half + spare
    query = dot(asking, weights[:, :span])
    key = dot(asked, weights[:, half - spare : 2 * half])
    value = dot(asked, weights[:, 2 * half : 2 * half + span])
    heads[:, :spare] = jnp.zeros((asking.shape[0], spare), F32)
    for head in range(half // HD):
        at = head * HD
        score = contract_last(
            query[:, at : at + HD].astype(BF), key[:, spare + at : spare + at + HD].astype(BF)
        )
        raw = jnp.exp(score * (1.0 / math.sqrt(HD))) * allowed
        share = (raw * (1.0 / jnp.sum(raw, axis=1, keepdims=True))).astype(BF)
        heads[:, spare + at : spare + at + HD] = dot(share, value[:, at : at + HD].astype(BF))
    return contract_last(heads[...].astype(BF), weights[:, 3 * half - spare : 4 * half]).astype(BF)


def split_rows(values, sub, keep, give, whole):
    rows = keep.shape[0]
    whole[...] = values
    keep[...] = whole[pl.ds(pl.multiple_of(sub * rows, 16), rows), :]
    give[...] = whole[pl.ds(pl.multiple_of((1 - sub) * rows, 16), rows), :]


def vision_block(at, part, info, values, weights_hbm, out, weights, heads, sem):
    base = at - at % 128
    load = pltpu.make_async_copy(weights_hbm.at[:, base : base + weights.shape[1]], weights, sem)
    load.start()
    rows = values.shape[0]

    def image_of(row):
        token = lax.rem(row, rows // 4)
        image = jnp.zeros(row.shape, jnp.int32)
        for step in range(info.shape[0]):
            image = image + jnp.where(token >= info[step], 1, 0)
        return image

    asking = image_of(lax.broadcasted_iota(jnp.int32, (rows, 1), 0))
    asked = image_of(lax.broadcasted_iota(jnp.int32, (1, rows), 1))
    allowed = jnp.where(asking == asked, 1.0, 0.0)
    heads[...] = jnp.zeros(heads.shape, F32)
    load.wait()
    triple = []
    for member in range(3):
        begin = at - base + member * part
        end = begin + part
        low = begin - begin % 128
        high = end + -end % 128
        triple.append((dot(values[...], weights[:, low:high]), begin - low))
    for head in range(part // HD):
        query, key, value = (
            array[:, shift + head * HD : shift + (head + 1) * HD].astype(BF)
            for array, shift in triple
        )
        raw = jnp.exp(contract_last(query, key) * (1.0 / math.sqrt(HD))) * allowed
        share = (raw * (1.0 / jnp.sum(raw, axis=1, keepdims=True))).astype(BF)
        heads[:, head * HD : (head + 1) * HD] = dot(share, value)
    out[...] = heads[...].astype(BF)


def run_vision_block(at, part, info, values, weights):
    rows, width = values.shape
    vmem = pl.BlockSpec(memory_space=pltpu.VMEM)
    end = at + 3 * part
    return pl.pallas_call(
        functools.partial(vision_block, at, part),
        out_shape=jax.ShapeDtypeStruct((rows, part + pad_to(part)), BF),
        in_specs=[pl.BlockSpec(memory_space=pltpu.SMEM), vmem]
        + [pl.BlockSpec(memory_space=pl.ANY)],
        out_specs=vmem,
        scratch_shapes=[
            pltpu.VMEM((width, end + pad_to(end) - (at - at % 128)), BF),
            pltpu.VMEM((rows, part + pad_to(part)), F32),
            pltpu.SemaphoreType.DMA,
        ],
        compiler_params=pltpu.CompilerParams(vmem_limit_bytes=56 << 20),
    )(info, values, weights)


def vision_output(at, part, info, own, other, weights_hbm, keep, give, weights, heads, whole, sem):
    base = at - at % 128
    load = pltpu.make_async_copy(weights_hbm.at[:, base : base + weights.shape[1]], weights, sem)
    load.start()
    heads[...] = jnp.zeros(heads.shape, F32)
    low = info[1] == 0
    begin = at - base
    mine = own[...].astype(F32)[:, :part]
    theirs = other[...].astype(F32)[:, :part]
    heads[:, begin : begin + part] = jnp.where(low, mine, theirs)
    heads[:, begin + part : begin + 2 * part] = jnp.where(low, theirs, mine)
    load.wait()
    partial = contract_last(heads[...].astype(BF), weights[...])
    split_rows(partial.astype(BF), info[0], keep, give, whole)


def run_vision_output(at, part, info, own, other, weights):
    rows = own.shape[0]
    width = weights.shape[0]
    end = at + 2 * part
    span = end + pad_to(end) - (at - at % 128)
    vmem = pl.BlockSpec(memory_space=pltpu.VMEM)
    return pl.pallas_call(
        functools.partial(vision_output, at, part),
        out_shape=[jax.ShapeDtypeStruct((rows // 2, width), BF)] * 2,
        in_specs=[pl.BlockSpec(memory_space=pltpu.SMEM), vmem, vmem]
        + [pl.BlockSpec(memory_space=pl.ANY)],
        out_specs=[vmem] * 2,
        scratch_shapes=[
            pltpu.VMEM((width, span), BF),
            pltpu.VMEM((rows, span), F32),
            pltpu.VMEM((rows, width), BF),
            pltpu.SemaphoreType.DMA,
        ],
        compiler_params=pltpu.CompilerParams(vmem_limit_bytes=56 << 20),
    )(info, own, other, weights)


def merger_rows(patches, keep, other, spread, out):
    hidden = patches[...].astype(F32) + (keep[...].astype(F32) + other[...].astype(F32))
    ready = dot(layer_norm(hidden).astype(BF), spread[...]).astype(BF)
    columns = out.shape[2]
    for place in range(out.shape[0]):
        out[place] = ready[:, place * columns : (place + 1) * columns]


def run_merger_rows(lines, patches, keep, other, spread):
    rows = patches.shape[0]
    vmem = pl.BlockSpec(memory_space=pltpu.VMEM)
    return pl.pallas_call(
        merger_rows,
        out_shape=jax.ShapeDtypeStruct((lines, rows, spread.shape[1] // lines), BF),
        in_specs=[vmem] * 4,
        out_specs=vmem,
        compiler_params=pltpu.CompilerParams(vmem_limit_bytes=56 << 20),
    )(patches, keep, other, spread)


def merger_dot(depth, info, mine, theirs, weights_hbm, out, weights, sem):
    load = pltpu.make_async_copy(weights_hbm.at[:, : weights.shape[1]], weights, sem)
    load.start()
    sub = info[0]
    lines, rows = mine.shape[:2]
    half_rows = rows // 2
    load.wait()
    total = jnp.zeros((lines * half_rows, weights.shape[1]), F32)
    for side, values in ((sub, mine), (1 - sub, theirs)):
        for step in range(2):
            part = values[:, step * half_rows : (step + 1) * half_rows, :]
            part = part.reshape(lines * half_rows, part.shape[2])[:, :depth]
            row = pl.multiple_of((2 * side + step) * depth, 16)
            total = total + dot(part, weights[pl.ds(row, depth), :])
    out[...] = total[:, : out.shape[1]].astype(BF)


def run_merger_dot(half, depth, info, mine, theirs, weights):
    lines, rows = mine.shape[:2]
    vmem = pl.BlockSpec(memory_space=pltpu.VMEM)
    return pl.pallas_call(
        functools.partial(merger_dot, depth),
        out_shape=jax.ShapeDtypeStruct((lines * rows // 2, half), BF),
        in_specs=[pl.BlockSpec(memory_space=pltpu.SMEM), vmem, vmem]
        + [pl.BlockSpec(memory_space=pl.ANY)],
        out_specs=vmem,
        scratch_shapes=[
            pltpu.VMEM((weights.shape[0], half + pad_to(half)), BF),
            pltpu.SemaphoreType.DMA,
        ],
        compiler_params=pltpu.CompilerParams(vmem_limit_bytes=56 << 20),
    )(info, mine, theirs, weights)


def run_decoder_block(half, cap, info, got, other, text, reorder, weights):
    rows, width = text.shape
    block = rows // (REACH + 1)
    vmem = pl.BlockSpec(memory_space=pltpu.VMEM)
    return pl.pallas_call(
        functools.partial(decoder_block, half, cap),
        out_shape=[jax.ShapeDtypeStruct((block // 2, width), BF)] * 2,
        in_specs=[pl.BlockSpec(memory_space=pltpu.SMEM)]
        + [vmem] * 4
        + [pl.BlockSpec(memory_space=pl.ANY)],
        out_specs=[vmem] * 2,
        scratch_shapes=[
            pltpu.VMEM(weights.shape, BF),
            pltpu.VMEM((block, half + half % 128), F32),
            pltpu.VMEM((block, width), BF),
            pltpu.SemaphoreType.DMA,
        ],
        compiler_params=pltpu.CompilerParams(vmem_limit_bytes=56 << 20),
    )(info, got, other, text, reorder, weights)


def shards(
    patches,
    image_sizes,
    vision_inproj,
    vision_outproj,
    merger_weight,
    text_embed,
    image_positions,
    prompt_lengths,
    decoder_inproj,
    decoder_outproj,
):
    lines = lax.axis_size("zh")
    planes = lax.axis_size(PLANE)
    pieces = lax.axis_size(TOK)
    rows_v, width = patches.shape
    half = vision_inproj.shape[3]
    krows = vision_inproj.shape[0]
    mrows = merger_weight.shape[0]

    group = lax.axis_index("grp")
    part = half // 2
    vin = vision_inproj.reshape(krows, 3, 2, part)
    vin = jnp.where(group == 0, vin[:, :, 0], vin[:, :, 1]).reshape(krows, 3 * part)
    line = jnp.concatenate([vin, vision_outproj.T], axis=1)
    line = to_all(line, "zh").reshape(lines * krows, 3 * part + half)
    at_in = half + pad_to(half)
    at_out = at_in + 3 * part
    end = at_out + half
    merge = jnp.pad(merger_weight, ((0, 0), (0, pad_to(half))))
    line_v = jnp.concatenate([merge, line, jnp.zeros((mrows, pad_to(end)), BF)], axis=1)

    drows = decoder_inproj.shape[0]
    dec = decoder_inproj.reshape(drows, 3 * half)
    dec = jnp.stack(
        [
            dec[:, : 2 * half],
            jnp.concatenate([dec[:, 2 * half :], decoder_outproj.T], axis=1),
        ]
    )
    dec_other = lax.ppermute(dec, "grp", [(0, 1), (1, 0)])
    low = lax.axis_index("grp") == 0
    dec = jnp.stack([jnp.where(low, dec, dec_other), jnp.where(low, dec_other, dec)], axis=1)
    dec = dec.reshape(4 * drows, width)
    tokens = rows_v // 4
    patches = patches.reshape(tokens, 4, width).transpose(1, 0, 2).reshape(rows_v, width)
    sub = lax.axis_index("sub")
    side_v = rows_v // 2
    own_patches = jnp.where(sub == 0, patches[:side_v], patches[side_v:])
    normed = layer_norm(patches.astype(F32)).astype(BF)
    ends = jnp.cumsum(image_sizes[0])
    mark = jnp.pad(ends.astype(BF)[None], ((0, 15), (0, width - ends.shape[0])))
    marked = jnp.concatenate([normed, mark], axis=0)
    depth = 4 * mrows
    spread_at = jnp.arange(lines * (depth + pad_to(depth)), dtype=jnp.int32)
    inner = spread_at % (depth + pad_to(depth))
    source = inner // mrows * (lines * mrows) + inner % mrows
    source = source + spread_at // (depth + pad_to(depth)) * mrows
    source = jnp.where(inner < depth, source, width)
    spread = (jnp.arange(width, dtype=jnp.int32)[:, None] == source[None, :]).astype(BF)
    me = lax.axis_index("zh")
    order = jnp.arange(width, dtype=jnp.int32)
    fan = 2 * drows
    natural = (
        order // drows % 2 * (width // 2)
        + order // (lines * fan) * (lines * drows)
        + (me - order // fan) % lines * drows
        + order % drows
    )
    reorder = (natural[None, :] == order[:, None]).astype(BF)
    first = lax.axis_index("sub") == 0
    side_t = text_embed.shape[0] // 2
    mine = jnp.concatenate(
        [
            jnp.where(first, text_embed[:side_t], text_embed[side_t:]),
            dec,
            jnp.zeros((-4 * drows % 16, width), BF),
        ],
        axis=0,
    )
    line_v, marked, reorder, mine, spread, own_patches = lax.optimization_barrier(
        (line_v, marked, reorder, mine, spread, own_patches)
    )
    full_v = lax.all_gather(line_v, PLANE, axis=0, tiled=True)

    piece_rows = text_embed.shape[0]
    reach = REACH + 1
    cap = rows_v // (2 * pieces)
    slots = reach * cap
    targets = image_positions[0]
    target_piece = targets // piece_rows
    target_row = targets % piece_rows
    hits = (target_piece[:, None] == jnp.arange(pieces, dtype=jnp.int32)[None, :]).astype(jnp.int32)
    slot = jnp.sum((jnp.cumsum(hits, axis=0) - hits) * hits, axis=1)
    dest = jnp.arange(pieces * slots, dtype=jnp.int32)
    back = dest // cap % reach
    wanted = (dest // slots)[:, None] - back[:, None] == target_piece[None, :]
    wanted = wanted & ((dest % cap)[:, None] == slot[None, :])
    window_rows = reach * piece_rows

    moved = [
        lax.ppermute(mine, "zh", [(i, (i + s) % lines) for i in range(lines)])
        for s in range(1, lines)
    ]
    line_d = jnp.stack([m[side_t : side_t + 4 * drows] for m in [mine] + moved])
    line_d = jnp.concatenate([line_d[:, : 2 * drows], line_d[:, 2 * drows :]], axis=2)
    full_d = lax.all_gather(
        line_d.reshape(lines * 2 * drows, 4 * half), PLANE, axis=0, tiled=True
    )

    text = jnp.stack([m[:side_t] for m in moved[::-1]])
    before = lax.ppermute(text, PLANE, [(i, i + 1) for i in range(planes - 1)])
    steps = jnp.arange(REACH, 0, -1, dtype=jnp.int32)[:, None, None]
    text = both_halves(jnp.where(steps <= me, text, before), first)
    window_text = jnp.concatenate([text.reshape(REACH * piece_rows, width), text_embed], axis=0)
    window_text = dot(window_text, reorder).astype(BF)

    place_info = jnp.stack([sub, group]).astype(jnp.int32)
    pair = [(0, 1), (1, 0)]
    paired = lax.ppermute(marked, "grp", pair)
    paired_ends = paired[rows_v, : ends.shape[0]].astype(jnp.int32)
    heads_away = run_vision_block(at_in, part, paired_ends, paired[:rows_v], full_v)
    heads = run_vision_block(at_in, part, ends, marked[:rows_v], full_v)
    heads_back = lax.ppermute(heads_away, "grp", pair)
    keep, give = run_vision_output(at_out, part, place_info, heads, heads_back, full_v)
    merged = run_merger_rows(lines, own_patches, keep, swap_sub(give), spread)
    merged = lax.all_to_all(merged, "zh", split_axis=0, concat_axis=0, tiled=True)
    partial = run_merger_dot(half, depth, place_info, merged, swap_sub(merged), full_v)
    partial = partial.reshape(lines, tokens, half)
    partial = lax.all_to_all(partial, "zh", split_axis=0, concat_axis=0, tiled=True)
    embedded = jnp.sum(partial.astype(F32), axis=0).astype(BF)

    note = jnp.stack([target_row, jnp.ones_like(target_row)], axis=1).astype(BF)
    note = jnp.pad(note, ((0, 0), (0, pad_to(half) - 2)))
    sent = dot(wanted.astype(BF), jnp.concatenate([embedded, note], axis=1)).astype(BF)
    got = lax.all_to_all(
        sent.reshape(pieces, slots, half + pad_to(half)), TOK, split_axis=0, concat_axis=0, tiled=True
    ).reshape(pieces * slots, half + pad_to(half))
    got, window_text = lax.optimization_barrier((got, window_text))
    lengths = prompt_lengths[0]
    starts = jnp.cumsum(lengths) - lengths
    info = jnp.concatenate(
        [jnp.stack([lax.axis_index("sub"), lax.axis_index(TOK)]).astype(jnp.int32), starts]
    )
    keep, give = run_decoder_block(
        half, cap, info, got, swap_sub(got), window_text, reorder, full_d
    )
    return (keep.astype(F32) + swap_sub(give).astype(F32)).astype(BF)


def solution(mesh):
    grp, tok, sub = mesh.devices.shape
    lined = Mesh(mesh.devices.reshape(grp, 4, 4, tok // 16, sub), ("grp", "y", "x", "zh", "sub"))
    whole = ("grp",) + TOK
    placed = (
        P(whole, None),
        P(whole, None),
        P(TOK, "sub", None, None),
        P("sub", TOK),
        P(TOK, "sub"),
        P(whole, None),
        P("grp", TOK),
        P("grp", None),
        P(whole, "sub", None, None),
        P("sub", whole),
    )
    return jax.shard_map(
        shards,
        mesh=lined,
        in_specs=placed,
        out_specs=P(whole + ("sub",), None),
        check_vma=False,
    )
```

```python
import functools
import math

import jax
import jax.numpy as jnp
from jax import lax
from jax.experimental import pallas as pl
from jax.experimental.pallas import tpu as pltpu
from jax.sharding import Mesh
from jax.sharding import PartitionSpec as P

HD = 88
REACH = 3
EPS = 1e-06
TOK = ("y", "x", "zh")
PLANE = ("y", "x")
BF = jnp.bfloat16
F32 = jnp.float32


def layer_norm(values):
    center = values - jnp.mean(values, axis=-1, keepdims=True)
    spread = jnp.mean(center * center, axis=-1, keepdims=True)
    return center * lax.rsqrt(spread + EPS)


def softmax_weights(scores, allowed):
    raw = jnp.exp(scores * (1.0 / math.sqrt(HD))) * allowed
    return (raw / jnp.sum(raw, axis=-1, keepdims=True)).astype(BF)


def swap_sub(value):
    return lax.ppermute(value, "sub", [(0, 1), (1, 0)])


def dot(a, b):
    return jnp.dot(a, b, preferred_element_type=F32)


def both_halves(part, first):
    return join_halves(part, swap_sub(part), first)


def join_halves(part, other, first):
    return jnp.concatenate(
        [jnp.where(first, part, other), jnp.where(first, other, part)], axis=1
    )


def pad_to(columns):
    return -columns % 128


def to_all(value, axes):
    count = lax.axis_size(axes)
    spread = jnp.broadcast_to(value[None], (count,) + value.shape)
    return lax.all_to_all(spread, axes, split_axis=0, concat_axis=0, tiled=True)


def contract_last(a, b):
    return lax.dot_general(a, b, (((1,), (1,)), ((), ())), preferred_element_type=F32)


def contract_first(a, b):
    return lax.dot_general(a, b, (((0,), (0,)), ((), ())), preferred_element_type=F32)


def decoder_block(
    half, cap, info, got, other, text, reorder, weights_hbm, keep, give, weights, heads, whole, sem
):
    load = pltpu.make_async_copy(weights_hbm, weights, sem)
    load.start()
    sub = info[0]
    piece = info[1]
    rows = text.shape[0]
    block = rows // (REACH + 1)
    tokens = got.shape[0]

    note = got[:, half - half % 128 :].astype(F32)
    spare = half % 128
    row = note[:, spare : spare + 1].astype(jnp.int32)
    flag = note[:, spare + 1 : spare + 2]
    index = lax.broadcasted_iota(jnp.int32, (tokens, 1), 0)
    back = lax.rem(lax.div(index, cap), REACH + 1)
    target = jnp.where(flag > 0.5, (REACH - back) * block + row, rows)
    place = lax.broadcasted_iota(jnp.int32, (tokens, rows), 1) == target
    place = jnp.where(place, 1.0, 0.0).astype(BF)
    mine = reorder[pl.ds(pl.multiple_of(sub * half, 16), half), :]
    theirs = reorder[pl.ds(pl.multiple_of((1 - sub) * half, 16), half), :]
    image = dot(got[:, :half], mine) + dot(other[:, :half], theirs)
    placed = contract_first(place, image.astype(BF))
    filled = contract_first(place, jnp.ones((tokens, 128), BF))
    values = jnp.where(filled[:, :1] > 0.5, placed, text[...].astype(F32))
    normed = layer_norm(values).astype(BF)

    load.wait()
    query_pos = piece * block + lax.broadcasted_iota(jnp.int32, (block, 1), 0)
    key_pos = (piece - REACH) * block + lax.broadcasted_iota(jnp.int32, (1, rows), 1)
    start = jnp.zeros((block, 1), jnp.int32)
    for prompt in range(2, info.shape[0]):
        start = jnp.where(query_pos >= info[prompt], jnp.maximum(start, info[prompt]), start)
    allowed = jnp.where((key_pos <= query_pos) & (key_pos >= start), 1.0, 0.0)
    partial = attention(half, normed[REACH * block :], normed, weights, heads, allowed)
    split_rows(contract_last(partial, reorder[...]).astype(BF), sub, keep, give, whole)


def attention(half, asking, asked, weights, heads, allowed):
    spare = half % 128
    span = half + spare
    query = dot(asking, weights[:, :span])
    key = dot(asked, weights[:, half - spare : 2 * half])
    value = dot(asked, weights[:, 2 * half : 2 * half + span])
    heads[:, :spare] = jnp.zeros((asking.shape[0], spare), F32)
    for head in range(half // HD):
        at = head * HD
        score = contract_last(
            query[:, at : at + HD].astype(BF), key[:, spare + at : spare + at + HD].astype(BF)
        )
        raw = jnp.exp(score * (1.0 / math.sqrt(HD))) * allowed
        share = (raw * (1.0 / jnp.sum(raw, axis=1, keepdims=True))).astype(BF)
        heads[:, spare + at : spare + at + HD] = dot(share, value[:, at : at + HD].astype(BF))
    return contract_last(heads[...].astype(BF), weights[:, 3 * half - spare : 4 * half]).astype(BF)


def split_rows(values, sub, keep, give, whole):
    rows = keep.shape[0]
    whole[...] = values
    keep[...] = whole[pl.ds(pl.multiple_of(sub * rows, 16), rows), :]
    give[...] = whole[pl.ds(pl.multiple_of((1 - sub) * rows, 16), rows), :]


def vision_block(at, part, info, values, weights_hbm, out, weights, heads, sem):
    base = at - at % 128
    load = pltpu.make_async_copy(weights_hbm.at[:, base : base + weights.shape[1]], weights, sem)
    load.start()
    rows = values.shape[0]

    def image_of(row):
        token = lax.rem(row, rows // 4)
        image = jnp.zeros(row.shape, jnp.int32)
        for step in range(info.shape[0]):
            image = image + jnp.where(token >= info[step], 1, 0)
        return image

    asking = image_of(lax.broadcasted_iota(jnp.int32, (rows, 1), 0))
    asked = image_of(lax.broadcasted_iota(jnp.int32, (1, rows), 1))
    allowed = jnp.where(asking == asked, 1.0, 0.0)
    heads[...] = jnp.zeros(heads.shape, F32)
    load.wait()
    triple = []
    for member in range(3):
        begin = at - base + member * part
        end = begin + part
        low = begin - begin % 128
        high = end + -end % 128
        triple.append((dot(values[...], weights[:, low:high]), begin - low))
    for head in range(part // HD):
        query, key, value = (
            array[:, shift + head * HD : shift + (head + 1) * HD].astype(BF)
            for array, shift in triple
        )
        raw = jnp.exp(contract_last(query, key) * (1.0 / math.sqrt(HD))) * allowed
        share = (raw * (1.0 / jnp.sum(raw, axis=1, keepdims=True))).astype(BF)
        heads[:, head * HD : (head + 1) * HD] = dot(share, value)
    out[...] = heads[...].astype(BF)


def run_vision_block(at, part, info, values, weights):
    rows, width = values.shape
    vmem = pl.BlockSpec(memory_space=pltpu.VMEM)
    end = at + 3 * part
    return pl.pallas_call(
        functools.partial(vision_block, at, part),
        out_shape=jax.ShapeDtypeStruct((rows, part + pad_to(part)), BF),
        in_specs=[pl.BlockSpec(memory_space=pltpu.SMEM), vmem]
        + [pl.BlockSpec(memory_space=pl.ANY)],
        out_specs=vmem,
        scratch_shapes=[
            pltpu.VMEM((width, end + pad_to(end) - (at - at % 128)), BF),
            pltpu.VMEM((rows, part + pad_to(part)), F32),
            pltpu.SemaphoreType.DMA,
        ],
        compiler_params=pltpu.CompilerParams(vmem_limit_bytes=56 << 20),
    )(info, values, weights)


def vision_output(at, part, info, own, other, weights_hbm, keep, give, weights, heads, whole, sem):
    base = at - at % 128
    load = pltpu.make_async_copy(weights_hbm.at[:, base : base + weights.shape[1]], weights, sem)
    load.start()
    heads[...] = jnp.zeros(heads.shape, F32)
    low = info[1] == 0
    begin = at - base
    mine = own[...].astype(F32)[:, :part]
    theirs = other[...].astype(F32)[:, :part]
    heads[:, begin : begin + part] = jnp.where(low, mine, theirs)
    heads[:, begin + part : begin + 2 * part] = jnp.where(low, theirs, mine)
    load.wait()
    partial = contract_last(heads[...].astype(BF), weights[...])
    split_rows(partial.astype(BF), info[0], keep, give, whole)


def run_vision_output(at, part, info, own, other, weights):
    rows = own.shape[0]
    width = weights.shape[0]
    end = at + 2 * part
    span = end + pad_to(end) - (at - at % 128)
    vmem = pl.BlockSpec(memory_space=pltpu.VMEM)
    return pl.pallas_call(
        functools.partial(vision_output, at, part),
        out_shape=[jax.ShapeDtypeStruct((rows // 2, width), BF)] * 2,
        in_specs=[pl.BlockSpec(memory_space=pltpu.SMEM), vmem, vmem]
        + [pl.BlockSpec(memory_space=pl.ANY)],
        out_specs=[vmem] * 2,
        scratch_shapes=[
            pltpu.VMEM((width, span), BF),
            pltpu.VMEM((rows, span), F32),
            pltpu.VMEM((rows, width), BF),
            pltpu.SemaphoreType.DMA,
        ],
        compiler_params=pltpu.CompilerParams(vmem_limit_bytes=56 << 20),
    )(info, own, other, weights)


def merger_rows(piece, patches, keep, other, out, ordered):
    hidden = patches[...].astype(F32) + (keep[...].astype(F32) + other[...].astype(F32))
    ready = layer_norm(hidden)
    lines = out.shape[0]
    count = ready.shape[1] // (lines * piece)
    ordered[...] = jnp.zeros(ordered.shape, F32)
    for place in range(lines):
        for part in range(count):
            source = (part * lines + place) * piece
            ordered[place, :, part * piece : (part + 1) * piece] = ready[
                :, source : source + piece
            ]
    out[...] = ordered[...].astype(BF)


def run_merger_rows(lines, piece, patches, keep, other):
    rows, width = patches.shape
    shape = (lines, rows, width // lines + pad_to(width // lines))
    vmem = pl.BlockSpec(memory_space=pltpu.VMEM)
    return pl.pallas_call(
        functools.partial(merger_rows, piece),
        out_shape=jax.ShapeDtypeStruct(shape, BF),
        in_specs=[vmem] * 3,
        out_specs=vmem,
        scratch_shapes=[pltpu.VMEM(shape, F32)],
        compiler_params=pltpu.CompilerParams(vmem_limit_bytes=56 << 20),
    )(patches, keep, other)


def merger_dot(depth, info, mine, theirs, weights_hbm, out, weights, sem):
    load = pltpu.make_async_copy(weights_hbm.at[:, : weights.shape[1]], weights, sem)
    load.start()
    sub = info[0]
    lines, rows = mine.shape[:2]
    half_rows = rows // 2
    load.wait()
    total = jnp.zeros((lines * half_rows, weights.shape[1]), F32)
    for side, values in ((sub, mine), (1 - sub, theirs)):
        for step in range(2):
            part = values[:, step * half_rows : (step + 1) * half_rows, :]
            part = part.reshape(lines * half_rows, part.shape[2])[:, :depth]
            row = pl.multiple_of((2 * side + step) * depth, 16)
            total = total + dot(part, weights[pl.ds(row, depth), :])
    out[...] = total[:, : out.shape[1]].astype(BF)


def run_merger_dot(half, depth, info, mine, theirs, weights):
    lines, rows = mine.shape[:2]
    vmem = pl.BlockSpec(memory_space=pltpu.VMEM)
    return pl.pallas_call(
        functools.partial(merger_dot, depth),
        out_shape=jax.ShapeDtypeStruct((lines * rows // 2, half), BF),
        in_specs=[pl.BlockSpec(memory_space=pltpu.SMEM), vmem, vmem]
        + [pl.BlockSpec(memory_space=pl.ANY)],
        out_specs=vmem,
        scratch_shapes=[
            pltpu.VMEM((weights.shape[0], half + pad_to(half)), BF),
            pltpu.SemaphoreType.DMA,
        ],
        compiler_params=pltpu.CompilerParams(vmem_limit_bytes=56 << 20),
    )(info, mine, theirs, weights)


def run_decoder_block(half, cap, info, got, other, text, reorder, weights):
    rows, width = text.shape
    block = rows // (REACH + 1)
    vmem = pl.BlockSpec(memory_space=pltpu.VMEM)
    return pl.pallas_call(
        functools.partial(decoder_block, half, cap),
        out_shape=[jax.ShapeDtypeStruct((block // 2, width), BF)] * 2,
        in_specs=[pl.BlockSpec(memory_space=pltpu.SMEM)]
        + [vmem] * 4
        + [pl.BlockSpec(memory_space=pl.ANY)],
        out_specs=[vmem] * 2,
        scratch_shapes=[
            pltpu.VMEM(weights.shape, BF),
            pltpu.VMEM((block, half + half % 128), F32),
            pltpu.VMEM((block, width), BF),
            pltpu.SemaphoreType.DMA,
        ],
        compiler_params=pltpu.CompilerParams(vmem_limit_bytes=56 << 20),
    )(info, got, other, text, reorder, weights)


def shards(
    patches,
    image_sizes,
    vision_inproj,
    vision_outproj,
    merger_weight,
    text_embed,
    image_positions,
    prompt_lengths,
    decoder_inproj,
    decoder_outproj,
):
    lines = lax.axis_size("zh")
    planes = lax.axis_size(PLANE)
    pieces = lax.axis_size(TOK)
    rows_v, width = patches.shape
    half = vision_inproj.shape[3]
    krows = vision_inproj.shape[0]
    mrows = merger_weight.shape[0]

    group = lax.axis_index("grp")
    part = half // 2
    vin = vision_inproj.reshape(krows, 3, 2, part)
    vin = jnp.where(group == 0, vin[:, :, 0], vin[:, :, 1]).reshape(krows, 3 * part)
    line = jnp.concatenate([vin, vision_outproj.T], axis=1)
    line = to_all(line, "zh").reshape(lines * krows, 3 * part + half)
    at_in = half + pad_to(half)
    at_out = at_in + 3 * part
    end = at_out + half
    merge = jnp.pad(merger_weight, ((0, 0), (0, pad_to(half))))
    line_v = jnp.concatenate([merge, line, jnp.zeros((mrows, pad_to(end)), BF)], axis=1)

    drows = decoder_inproj.shape[0]
    dec = decoder_inproj.reshape(drows, 3 * half)
    dec = jnp.stack(
        [
            dec[:, : 2 * half],
            jnp.concatenate([dec[:, 2 * half :], decoder_outproj.T], axis=1),
        ]
    )
    dec_other = lax.ppermute(dec, "grp", [(0, 1), (1, 0)])
    low = lax.axis_index("grp") == 0
    dec = jnp.stack([jnp.where(low, dec, dec_other), jnp.where(low, dec_other, dec)], axis=1)
    dec = dec.reshape(4 * drows, width)
    tokens = rows_v // 4
    patches = patches.reshape(tokens, 4, width).transpose(1, 0, 2).reshape(rows_v, width)
    sub = lax.axis_index("sub")
    side_v = rows_v // 2
    own_patches = jnp.where(sub == 0, patches[:side_v], patches[side_v:])
    normed = layer_norm(patches.astype(F32)).astype(BF)
    ends = jnp.cumsum(image_sizes[0])
    mark = jnp.pad(ends.astype(BF)[None], ((0, 15), (0, width - ends.shape[0])))
    marked = jnp.concatenate([normed, mark], axis=0)
    depth = 4 * mrows
    me = lax.axis_index("zh")
    order = jnp.arange(width, dtype=jnp.int32)
    fan = 2 * drows
    natural = (
        order // drows % 2 * (width // 2)
        + order // (lines * fan) * (lines * drows)
        + (me - order // fan) % lines * drows
        + order % drows
    )
    reorder = (natural[None, :] == order[:, None]).astype(BF)
    first = lax.axis_index("sub") == 0
    side_t = text_embed.shape[0] // 2
    mine = jnp.concatenate(
        [
            jnp.where(first, text_embed[:side_t], text_embed[side_t:]),
            dec,
            jnp.zeros((-4 * drows % 16, width), BF),
        ],
        axis=0,
    )
    line_v, marked, reorder, mine, own_patches = lax.optimization_barrier(
        (line_v, marked, reorder, mine, own_patches)
    )
    full_v = lax.all_gather(line_v, PLANE, axis=0, tiled=True)

    piece_rows = text_embed.shape[0]
    reach = REACH + 1
    cap = rows_v // (2 * pieces)
    slots = reach * cap
    targets = image_positions[0]
    target_piece = targets // piece_rows
    target_row = targets % piece_rows
    hits = (target_piece[:, None] == jnp.arange(pieces, dtype=jnp.int32)[None, :]).astype(jnp.int32)
    slot = jnp.sum((jnp.cumsum(hits, axis=0) - hits) * hits, axis=1)
    dest = jnp.arange(pieces * slots, dtype=jnp.int32)
    back = dest // cap % reach
    wanted = (dest // slots)[:, None] - back[:, None] == target_piece[None, :]
    wanted = wanted & ((dest % cap)[:, None] == slot[None, :])
    window_rows = reach * piece_rows

    moved = [
        lax.ppermute(mine, "zh", [(i, (i + s) % lines) for i in range(lines)])
        for s in range(1, lines)
    ]
    line_d = jnp.stack([m[side_t : side_t + 4 * drows] for m in [mine] + moved])
    line_d = jnp.concatenate([line_d[:, : 2 * drows], line_d[:, 2 * drows :]], axis=2)
    full_d = lax.all_gather(
        line_d.reshape(lines * 2 * drows, 4 * half), PLANE, axis=0, tiled=True
    )

    text = jnp.stack([m[:side_t] for m in moved[::-1]])
    before = lax.ppermute(text, PLANE, [(i, i + 1) for i in range(planes - 1)])
    steps = jnp.arange(REACH, 0, -1, dtype=jnp.int32)[:, None, None]
    text = both_halves(jnp.where(steps <= me, text, before), first)
    window_text = jnp.concatenate([text.reshape(REACH * piece_rows, width), text_embed], axis=0)
    window_text = dot(window_text, reorder).astype(BF)

    place_info = jnp.stack([sub, group]).astype(jnp.int32)
    pair = [(0, 1), (1, 0)]
    paired = lax.ppermute(marked, "grp", pair)
    paired_ends = paired[rows_v, : ends.shape[0]].astype(jnp.int32)
    heads_away = run_vision_block(at_in, part, paired_ends, paired[:rows_v], full_v)
    heads = run_vision_block(at_in, part, ends, marked[:rows_v], full_v)
    heads_back = lax.ppermute(heads_away, "grp", pair)
    keep, give = run_vision_output(at_out, part, place_info, heads, heads_back, full_v)
    merged = run_merger_rows(lines, mrows, own_patches, keep, swap_sub(give))
    merged = lax.all_to_all(merged, "zh", split_axis=0, concat_axis=0, tiled=True)
    partial = run_merger_dot(half, depth, place_info, merged, swap_sub(merged), full_v)
    partial = partial.reshape(lines, tokens, half)
    partial = lax.all_to_all(partial, "zh", split_axis=0, concat_axis=0, tiled=True)
    embedded = jnp.sum(partial.astype(F32), axis=0).astype(BF)

    note = jnp.stack([target_row, jnp.ones_like(target_row)], axis=1).astype(BF)
    note = jnp.pad(note, ((0, 0), (0, pad_to(half) - 2)))
    sent = dot(wanted.astype(BF), jnp.concatenate([embedded, note], axis=1)).astype(BF)
    got = lax.all_to_all(
        sent.reshape(pieces, slots, half + pad_to(half)), TOK, split_axis=0, concat_axis=0, tiled=True
    ).reshape(pieces * slots, half + pad_to(half))
    got, window_text = lax.optimization_barrier((got, window_text))
    lengths = prompt_lengths[0]
    starts = jnp.cumsum(lengths) - lengths
    info = jnp.concatenate(
        [jnp.stack([lax.axis_index("sub"), lax.axis_index(TOK)]).astype(jnp.int32), starts]
    )
    keep, give = run_decoder_block(
        half, cap, info, got, swap_sub(got), window_text, reorder, full_d
    )
    return (keep.astype(F32) + swap_sub(give).astype(F32)).astype(BF)


def solution(mesh):
    grp, tok, sub = mesh.devices.shape
    lined = Mesh(mesh.devices.reshape(grp, 4, 4, tok // 16, sub), ("grp", "y", "x", "zh", "sub"))
    whole = ("grp",) + TOK
    placed = (
        P(whole, None),
        P(whole, None),
        P(TOK, "sub", None, None),
        P("sub", TOK),
        P(TOK, "sub"),
        P(whole, None),
        P("grp", TOK),
        P("grp", None),
        P(whole, "sub", None, None),
        P("sub", whole),
    )
    return jax.shard_map(
        shards,
        mesh=lined,
        in_specs=placed,
        out_specs=P(whole + ("sub",), None),
        check_vma=False,
    )
```

```python
import functools
import math

import jax
import jax.numpy as jnp
from jax import lax
from jax.experimental import pallas as pl
from jax.experimental.pallas import tpu as pltpu
from jax.sharding import Mesh
from jax.sharding import PartitionSpec as P

HD = 88
REACH = 3
EPS = 1e-06
TOK = ("y", "x", "zh")
PLANE = ("y", "x")
BF = jnp.bfloat16
F32 = jnp.float32


def layer_norm(values):
    center = values - jnp.mean(values, axis=-1, keepdims=True)
    spread = jnp.mean(center * center, axis=-1, keepdims=True)
    return center * lax.rsqrt(spread + EPS)


def softmax_weights(scores, allowed):
    raw = jnp.exp(scores * (1.0 / math.sqrt(HD))) * allowed
    return (raw / jnp.sum(raw, axis=-1, keepdims=True)).astype(BF)


def swap_sub(value):
    return lax.ppermute(value, "sub", [(0, 1), (1, 0)])


def dot(a, b):
    return jnp.dot(a, b, preferred_element_type=F32)


def both_halves(part, first):
    return join_halves(part, swap_sub(part), first)


def join_halves(part, other, first):
    return jnp.concatenate(
        [jnp.where(first, part, other), jnp.where(first, other, part)], axis=1
    )


def pad_to(columns):
    return -columns % 128


def to_all(value, axes):
    count = lax.axis_size(axes)
    spread = jnp.broadcast_to(value[None], (count,) + value.shape)
    return lax.all_to_all(spread, axes, split_axis=0, concat_axis=0, tiled=True)


def contract_last(a, b):
    return lax.dot_general(a, b, (((1,), (1,)), ((), ())), preferred_element_type=F32)


def contract_first(a, b):
    return lax.dot_general(a, b, (((0,), (0,)), ((), ())), preferred_element_type=F32)


def decoder_block(
    half, cap, info, got, other, text, reorder, weights_hbm, keep, give, weights, heads, whole, sem
):
    load = pltpu.make_async_copy(weights_hbm, weights, sem)
    load.start()
    sub = info[0]
    piece = info[1]
    rows = text.shape[0]
    block = rows // (REACH + 1)
    tokens = got.shape[0]

    note = got[:, half - half % 128 :].astype(F32)
    spare = half % 128
    row = note[:, spare : spare + 1].astype(jnp.int32)
    flag = note[:, spare + 1 : spare + 2]
    index = lax.broadcasted_iota(jnp.int32, (tokens, 1), 0)
    back = lax.rem(lax.div(index, cap), REACH + 1)
    target = jnp.where(flag > 0.5, (REACH - back) * block + row, rows)
    place = lax.broadcasted_iota(jnp.int32, (tokens, rows), 1) == target
    place = jnp.where(place, 1.0, 0.0).astype(BF)
    mine = reorder[pl.ds(pl.multiple_of(sub * half, 16), half), :]
    theirs = reorder[pl.ds(pl.multiple_of((1 - sub) * half, 16), half), :]
    image = dot(got[:, :half], mine) + dot(other[:, :half], theirs)
    placed = contract_first(place, image.astype(BF))
    filled = contract_first(place, jnp.ones((tokens, 128), BF))
    values = jnp.where(filled[:, :1] > 0.5, placed, text[...].astype(F32))
    normed = layer_norm(values).astype(BF)

    load.wait()
    query_pos = piece * block + lax.broadcasted_iota(jnp.int32, (block, 1), 0)
    key_pos = (piece - REACH) * block + lax.broadcasted_iota(jnp.int32, (1, rows), 1)
    start = jnp.zeros((block, 1), jnp.int32)
    for prompt in range(2, info.shape[0]):
        start = jnp.where(query_pos >= info[prompt], jnp.maximum(start, info[prompt]), start)
    allowed = jnp.where((key_pos <= query_pos) & (key_pos >= start), 1.0, 0.0)
    partial = attention(half, normed[REACH * block :], normed, weights, heads, allowed)
    split_rows(contract_last(partial, reorder[...]).astype(BF), sub, keep, give, whole)


def attention(half, asking, asked, weights, heads, allowed):
    spare = half % 128
    span = half + spare
    query = dot(asking, weights[:, :span])
    key = dot(asked, weights[:, half - spare : 2 * half])
    value = dot(asked, weights[:, 2 * half : 2 * half + span])
    heads[:, :spare] = jnp.zeros((asking.shape[0], spare), F32)
    for head in range(half // HD):
        at = head * HD
        score = contract_last(
            query[:, at : at + HD].astype(BF), key[:, spare + at : spare + at + HD].astype(BF)
        )
        raw = jnp.exp(score * (1.0 / math.sqrt(HD))) * allowed
        share = (raw * (1.0 / jnp.sum(raw, axis=1, keepdims=True))).astype(BF)
        heads[:, spare + at : spare + at + HD] = dot(share, value[:, at : at + HD].astype(BF))
    return contract_last(heads[...].astype(BF), weights[:, 3 * half - spare : 4 * half]).astype(BF)


def split_rows(values, sub, keep, give, whole):
    rows = keep.shape[0]
    whole[...] = values
    keep[...] = whole[pl.ds(pl.multiple_of(sub * rows, 16), rows), :]
    give[...] = whole[pl.ds(pl.multiple_of((1 - sub) * rows, 16), rows), :]


def vision_block(at, part, info, values, weights_hbm, out, weights, heads, sem):
    base = at - at % 128
    cut = at - base + 2 * part
    cut = cut + -cut % 128
    span = weights.shape[1]
    early = pltpu.make_async_copy(
        weights_hbm.at[:, base : base + cut], weights.at[:, :cut], sem.at[0]
    )
    late = pltpu.make_async_copy(
        weights_hbm.at[:, base + cut : base + span], weights.at[:, cut:], sem.at[1]
    )
    early.start()
    late.start()
    rows = values.shape[0]

    def image_of(row):
        token = lax.rem(row, rows // 4)
        image = jnp.zeros(row.shape, jnp.int32)
        for step in range(info.shape[0]):
            image = image + jnp.where(token >= info[step], 1, 0)
        return image

    asking = image_of(lax.broadcasted_iota(jnp.int32, (rows, 1), 0))
    asked = image_of(lax.broadcasted_iota(jnp.int32, (1, rows), 1))
    allowed = jnp.where(asking == asked, 1.0, 0.0)
    heads[...] = jnp.zeros(heads.shape, F32)
    early.wait()
    triple = []
    for member in range(3):
        if member == 2:
            late.wait()
        begin = at - base + member * part
        end = begin + part
        low = begin - begin % 128
        high = end + -end % 128
        triple.append((dot(values[...], weights[:, low:high]), begin - low))
    for head in range(part // HD):
        query, key, value = (
            array[:, shift + head * HD : shift + (head + 1) * HD].astype(BF)
            for array, shift in triple
        )
        raw = jnp.exp(contract_last(query, key) * (1.0 / math.sqrt(HD))) * allowed
        share = (raw * (1.0 / jnp.sum(raw, axis=1, keepdims=True))).astype(BF)
        heads[:, head * HD : (head + 1) * HD] = dot(share, value)
    out[...] = heads[...].astype(BF)


def run_vision_block(at, part, info, values, weights):
    rows, width = values.shape
    vmem = pl.BlockSpec(memory_space=pltpu.VMEM)
    end = at + 3 * part
    return pl.pallas_call(
        functools.partial(vision_block, at, part),
        out_shape=jax.ShapeDtypeStruct((rows, part + pad_to(part)), BF),
        in_specs=[pl.BlockSpec(memory_space=pltpu.SMEM), vmem]
        + [pl.BlockSpec(memory_space=pl.ANY)],
        out_specs=vmem,
        scratch_shapes=[
            pltpu.VMEM((width, end + pad_to(end) - (at - at % 128)), BF),
            pltpu.VMEM((rows, part + pad_to(part)), F32),
            pltpu.SemaphoreType.DMA((2,)),
        ],
        compiler_params=pltpu.CompilerParams(vmem_limit_bytes=56 << 20),
    )(info, values, weights)


def vision_output(at, part, info, own, other, weights_hbm, keep, give, weights, heads, whole, sem):
    base = at - at % 128
    load = pltpu.make_async_copy(weights_hbm.at[:, base : base + weights.shape[1]], weights, sem)
    load.start()
    heads[...] = jnp.zeros(heads.shape, F32)
    low = info[1] == 0
    begin = at - base
    mine = own[...].astype(F32)[:, :part]
    theirs = other[...].astype(F32)[:, :part]
    heads[:, begin : begin + part] = jnp.where(low, mine, theirs)
    heads[:, begin + part : begin + 2 * part] = jnp.where(low, theirs, mine)
    load.wait()
    partial = contract_last(heads[...].astype(BF), weights[...])
    split_rows(partial.astype(BF), info[0], keep, give, whole)


def run_vision_output(at, part, info, own, other, weights):
    rows = own.shape[0]
    width = weights.shape[0]
    end = at + 2 * part
    span = end + pad_to(end) - (at - at % 128)
    vmem = pl.BlockSpec(memory_space=pltpu.VMEM)
    return pl.pallas_call(
        functools.partial(vision_output, at, part),
        out_shape=[jax.ShapeDtypeStruct((rows // 2, width), BF)] * 2,
        in_specs=[pl.BlockSpec(memory_space=pltpu.SMEM), vmem, vmem]
        + [pl.BlockSpec(memory_space=pl.ANY)],
        out_specs=[vmem] * 2,
        scratch_shapes=[
            pltpu.VMEM((width, span), BF),
            pltpu.VMEM((rows, span), F32),
            pltpu.VMEM((rows, width), BF),
            pltpu.SemaphoreType.DMA,
        ],
        compiler_params=pltpu.CompilerParams(vmem_limit_bytes=56 << 20),
    )(info, own, other, weights)


def merger_rows(piece, patches, keep, other, out, ordered):
    hidden = patches[...].astype(F32) + (keep[...].astype(F32) + other[...].astype(F32))
    ready = layer_norm(hidden)
    lines = out.shape[0]
    count = ready.shape[1] // (lines * piece)
    ordered[...] = jnp.zeros(ordered.shape, F32)
    for place in range(lines):
        for part in range(count):
            source = (part * lines + place) * piece
            ordered[place, :, part * piece : (part + 1) * piece] = ready[
                :, source : source + piece
            ]
    out[...] = ordered[...].astype(BF)


def run_merger_rows(lines, piece, patches, keep, other):
    rows, width = patches.shape
    shape = (lines, rows, width // lines + pad_to(width // lines))
    vmem = pl.BlockSpec(memory_space=pltpu.VMEM)
    return pl.pallas_call(
        functools.partial(merger_rows, piece),
        out_shape=jax.ShapeDtypeStruct(shape, BF),
        in_specs=[vmem] * 3,
        out_specs=vmem,
        scratch_shapes=[pltpu.VMEM(shape, F32)],
        compiler_params=pltpu.CompilerParams(vmem_limit_bytes=56 << 20),
    )(patches, keep, other)


def merger_dot(depth, info, mine, theirs, weights_hbm, out, weights, sem):
    load = pltpu.make_async_copy(weights_hbm.at[:, : weights.shape[1]], weights, sem)
    load.start()
    sub = info[0]
    lines, rows = mine.shape[:2]
    half_rows = rows // 2
    load.wait()
    total = jnp.zeros((lines * half_rows, weights.shape[1]), F32)
    for side, values in ((sub, mine), (1 - sub, theirs)):
        for step in range(2):
            part = values[:, step * half_rows : (step + 1) * half_rows, :]
            part = part.reshape(lines * half_rows, part.shape[2])[:, :depth]
            row = pl.multiple_of((2 * side + step) * depth, 16)
            total = total + dot(part, weights[pl.ds(row, depth), :])
    out[...] = total[:, : out.shape[1]].astype(BF)


def run_merger_dot(half, depth, info, mine, theirs, weights):
    lines, rows = mine.shape[:2]
    vmem = pl.BlockSpec(memory_space=pltpu.VMEM)
    return pl.pallas_call(
        functools.partial(merger_dot, depth),
        out_shape=jax.ShapeDtypeStruct((lines * rows // 2, half), BF),
        in_specs=[pl.BlockSpec(memory_space=pltpu.SMEM), vmem, vmem]
        + [pl.BlockSpec(memory_space=pl.ANY)],
        out_specs=vmem,
        scratch_shapes=[
            pltpu.VMEM((weights.shape[0], half + pad_to(half)), BF),
            pltpu.SemaphoreType.DMA,
        ],
        compiler_params=pltpu.CompilerParams(vmem_limit_bytes=56 << 20),
    )(info, mine, theirs, weights)


def run_decoder_block(half, cap, info, got, other, text, reorder, weights):
    rows, width = text.shape
    block = rows // (REACH + 1)
    vmem = pl.BlockSpec(memory_space=pltpu.VMEM)
    return pl.pallas_call(
        functools.partial(decoder_block, half, cap),
        out_shape=[jax.ShapeDtypeStruct((block // 2, width), BF)] * 2,
        in_specs=[pl.BlockSpec(memory_space=pltpu.SMEM)]
        + [vmem] * 4
        + [pl.BlockSpec(memory_space=pl.ANY)],
        out_specs=[vmem] * 2,
        scratch_shapes=[
            pltpu.VMEM(weights.shape, BF),
            pltpu.VMEM((block, half + half % 128), F32),
            pltpu.VMEM((block, width), BF),
            pltpu.SemaphoreType.DMA,
        ],
        compiler_params=pltpu.CompilerParams(vmem_limit_bytes=56 << 20),
    )(info, got, other, text, reorder, weights)


def shards(
    patches,
    image_sizes,
    vision_inproj,
    vision_outproj,
    merger_weight,
    text_embed,
    image_positions,
    prompt_lengths,
    decoder_inproj,
    decoder_outproj,
):
    lines = lax.axis_size("zh")
    planes = lax.axis_size(PLANE)
    pieces = lax.axis_size(TOK)
    rows_v, width = patches.shape
    half = vision_inproj.shape[3]
    krows = vision_inproj.shape[0]
    mrows = merger_weight.shape[0]

    group = lax.axis_index("grp")
    part = half // 2
    vin = vision_inproj.reshape(krows, 3, 2, part)
    vin = jnp.where(group == 0, vin[:, :, 0], vin[:, :, 1]).reshape(krows, 3 * part)
    line = jnp.concatenate([vin, vision_outproj.T], axis=1)
    line = to_all(line, "zh").reshape(lines * krows, 3 * part + half)
    at_in = half + pad_to(half)
    at_out = at_in + 3 * part
    end = at_out + half
    merge = jnp.pad(merger_weight, ((0, 0), (0, pad_to(half))))
    line_v = jnp.concatenate([merge, line, jnp.zeros((mrows, pad_to(end)), BF)], axis=1)

    drows = decoder_inproj.shape[0]
    dec = decoder_inproj.reshape(drows, 3 * half)
    dec = jnp.stack(
        [
            dec[:, : 2 * half],
            jnp.concatenate([dec[:, 2 * half :], decoder_outproj.T], axis=1),
        ]
    )
    dec_other = lax.ppermute(dec, "grp", [(0, 1), (1, 0)])
    low = lax.axis_index("grp") == 0
    dec = jnp.stack([jnp.where(low, dec, dec_other), jnp.where(low, dec_other, dec)], axis=1)
    dec = dec.reshape(4 * drows, width)
    tokens = rows_v // 4
    patches = patches.reshape(tokens, 4, width).transpose(1, 0, 2).reshape(rows_v, width)
    sub = lax.axis_index("sub")
    side_v = rows_v // 2
    own_patches = jnp.where(sub == 0, patches[:side_v], patches[side_v:])
    normed = layer_norm(patches.astype(F32)).astype(BF)
    ends = jnp.cumsum(image_sizes[0])
    mark = jnp.pad(ends.astype(BF)[None], ((0, 15), (0, width - ends.shape[0])))
    marked = jnp.concatenate([normed, mark], axis=0)
    depth = 4 * mrows
    me = lax.axis_index("zh")
    order = jnp.arange(width, dtype=jnp.int32)
    fan = 2 * drows
    natural = (
        order // drows % 2 * (width // 2)
        + order // (lines * fan) * (lines * drows)
        + (me - order // fan) % lines * drows
        + order % drows
    )
    reorder = (natural[None, :] == order[:, None]).astype(BF)
    first = lax.axis_index("sub") == 0
    side_t = text_embed.shape[0] // 2
    mine = jnp.concatenate(
        [
            jnp.where(first, text_embed[:side_t], text_embed[side_t:]),
            dec,
            jnp.zeros((-4 * drows % 16, width), BF),
        ],
        axis=0,
    )
    line_v, marked, reorder, mine, own_patches = lax.optimization_barrier(
        (line_v, marked, reorder, mine, own_patches)
    )
    full_v = lax.all_gather(line_v, PLANE, axis=0, tiled=True)

    piece_rows = text_embed.shape[0]
    reach = REACH + 1
    cap = rows_v // (2 * pieces)
    slots = reach * cap
    targets = image_positions[0]
    target_piece = targets // piece_rows
    target_row = targets % piece_rows
    hits = (target_piece[:, None] == jnp.arange(pieces, dtype=jnp.int32)[None, :]).astype(jnp.int32)
    slot = jnp.sum((jnp.cumsum(hits, axis=0) - hits) * hits, axis=1)
    dest = jnp.arange(pieces * slots, dtype=jnp.int32)
    back = dest // cap % reach
    wanted = (dest // slots)[:, None] - back[:, None] == target_piece[None, :]
    wanted = wanted & ((dest % cap)[:, None] == slot[None, :])
    window_rows = reach * piece_rows

    moved = [
        lax.ppermute(mine, "zh", [(i, (i + s) % lines) for i in range(lines)])
        for s in range(1, lines)
    ]
    line_d = jnp.stack([m[side_t : side_t + 4 * drows] for m in [mine] + moved])
    line_d = jnp.concatenate([line_d[:, : 2 * drows], line_d[:, 2 * drows :]], axis=2)
    full_d = lax.all_gather(
        line_d.reshape(lines * 2 * drows, 4 * half), PLANE, axis=0, tiled=True
    )

    text = jnp.stack([m[:side_t] for m in moved[::-1]])
    before = lax.ppermute(text, PLANE, [(i, i + 1) for i in range(planes - 1)])
    steps = jnp.arange(REACH, 0, -1, dtype=jnp.int32)[:, None, None]
    text = both_halves(jnp.where(steps <= me, text, before), first)
    window_text = jnp.concatenate([text.reshape(REACH * piece_rows, width), text_embed], axis=0)
    window_text = dot(window_text, reorder).astype(BF)

    place_info = jnp.stack([sub, group]).astype(jnp.int32)
    pair = [(0, 1), (1, 0)]
    paired = lax.ppermute(marked, "grp", pair)
    paired_ends = paired[rows_v, : ends.shape[0]].astype(jnp.int32)
    heads_away = run_vision_block(at_in, part, paired_ends, paired[:rows_v], full_v)
    heads = run_vision_block(at_in, part, ends, marked[:rows_v], full_v)
    heads_back = lax.ppermute(heads_away, "grp", pair)
    keep, give = run_vision_output(at_out, part, place_info, heads, heads_back, full_v)
    merged = run_merger_rows(lines, mrows, own_patches, keep, swap_sub(give))
    merged = lax.all_to_all(merged, "zh", split_axis=0, concat_axis=0, tiled=True)
    partial = run_merger_dot(half, depth, place_info, merged, swap_sub(merged), full_v)
    partial = partial.reshape(lines, tokens, half)
    partial = lax.all_to_all(partial, "zh", split_axis=0, concat_axis=0, tiled=True)
    embedded = jnp.sum(partial.astype(F32), axis=0).astype(BF)

    note = jnp.stack([target_row, jnp.ones_like(target_row)], axis=1).astype(BF)
    note = jnp.pad(note, ((0, 0), (0, pad_to(half) - 2)))
    sent = dot(wanted.astype(BF), jnp.concatenate([embedded, note], axis=1)).astype(BF)
    got = lax.all_to_all(
        sent.reshape(pieces, slots, half + pad_to(half)), TOK, split_axis=0, concat_axis=0, tiled=True
    ).reshape(pieces * slots, half + pad_to(half))
    got, window_text = lax.optimization_barrier((got, window_text))
    lengths = prompt_lengths[0]
    starts = jnp.cumsum(lengths) - lengths
    info = jnp.concatenate(
        [jnp.stack([lax.axis_index("sub"), lax.axis_index(TOK)]).astype(jnp.int32), starts]
    )
    keep, give = run_decoder_block(
        half, cap, info, got, swap_sub(got), window_text, reorder, full_d
    )
    return (keep.astype(F32) + swap_sub(give).astype(F32)).astype(BF)


def solution(mesh):
    grp, tok, sub = mesh.devices.shape
    lined = Mesh(mesh.devices.reshape(grp, 4, 4, tok // 16, sub), ("grp", "y", "x", "zh", "sub"))
    whole = ("grp",) + TOK
    placed = (
        P(whole, None),
        P(whole, None),
        P(TOK, "sub", None, None),
        P("sub", TOK),
        P(TOK, "sub"),
        P(whole, None),
        P("grp", TOK),
        P("grp", None),
        P(whole, "sub", None, None),
        P("sub", whole),
    )
    return jax.shard_map(
        shards,
        mesh=lined,
        in_specs=placed,
        out_specs=P(whole + ("sub",), None),
        check_vma=False,
    )
```
